32 devices in a mesh: val: 4 (over x, core), cond: 8 (over z, y).
Axes of the slice: x: 2, y: 2, z: 4, core: 2. Of those that a mesh axis runs over, the one named last changes fastest.
Arguments:
- val_orbitals: bfloat16 [16, 768], P('val'), may hold values from -6 to 6
- cond_orbitals: bfloat16 [64, 768], P('cond'), may hold values from -6 to 6
- val_energy: bfloat16 [16], P('val'), may hold values from -0.59765625 to -0.049804688
- cond_energy: bfloat16 [64], P('cond'), may hold values from 0.049804688 to 1.1953125
- wave_index: int32 [4096], P('cond'), may hold values from 0 to 884735
Outputs:
- chi_real: float32 [128, 4096], P('val', 'cond')
- chi_imag: float32 [128, 4096], P('val', 'cond')
The draws below stay inside these ranges and needn't reach their ends.
Inputs may be any that keep to these rules, and one draw needn't show every extreme that they name: `wave_index`: values may repeat.
All inputs are finite; a program needn't handle non-finite values.
Results may differ from the reference program's by a relative error of at most 0.0037.
Values may be sent and summed in bfloat16 or wider, within the bound.
A program may use at most 64 MiB of HBM per device.

```python
import math
import jax
import jax.numpy as jnp
from jax import lax

NG = 96
NPW = 4096
NW = 128
SLAB_Y = 4
NPTS = 768
NVAL = 16
NCOND = 64


def set_ends(values, own_key, low, high):
    index_at = [jax.random.randint(jax.random.fold_in(own_key, axis), (), 0, length) for axis, length in enumerate(values.shape)]
    widest = values.shape.index(max(values.shape))
    next_to = index_at[:widest] + [(index_at[widest] + 1) % values.shape[widest]] + index_at[widest + 1:]
    return values.at[tuple(index_at)].set(low).at[tuple(next_to)].set(high)


def levels(rng, extent, pieces, low, largest):
    factor_of = 1.0
    for dim, shards_of in pieces:
        draws = jax.random.uniform(jax.random.fold_in(jax.random.fold_in(rng, 6), dim), (shards_of,), jnp.float32, low / len(pieces), largest / len(pieces))
        factor_of = factor_of * jnp.repeat(jnp.exp(draws), extent[dim] // shards_of).reshape((-1,) + (1,) * (len(extent) - 1 - dim))
    return factor_of


def bell_draw(key, shape, scale, limit, cuts=(), held_as=jnp.bfloat16):
    drawn = scale * jax.random.normal(key, shape, jnp.float32)
    if cuts:
        drawn = drawn * levels(key, shape, cuts, -0.22, 0.18)
    return jnp.clip(drawn, -limit, limit).astype(held_as)


def setup_inputs(seed: int = 0) -> dict:
    keys = jax.random.split(jax.random.key(seed), 6)
    return {
        "val_orbitals": bell_draw(keys[0], (NVAL, NPTS), 1.0, 6.0, ((0, 4),)),
        "cond_orbitals": bell_draw(keys[1], (NCOND, NPTS), 1.0, 6.0, ((0, 8),)),
        "val_energy": jnp.clip(-0.59765625 + 0.54785156 * jax.random.uniform(keys[2], (NVAL,), jnp.float32) ** levels(keys[2], (NVAL,), ((0, 4),), -0.2, 0.2), -0.59765625, -0.049804688).astype(jnp.bfloat16),
        "cond_energy": jnp.clip(0.049804688 + 1.1455078 * jax.random.uniform(keys[3], (NCOND,), jnp.float32) ** levels(keys[3], (NCOND,), ((0, 8),), -0.2, 0.2), 0.049804688, 1.1953125).astype(jnp.bfloat16),
        "wave_index": set_ends(jax.random.randint(keys[4], (NPW,), 0, NG * NG * NG), jax.random.fold_in(keys[4], 1), 0, (NG * NG * NG) - 1).astype(jnp.int32),
    }


def phase_table(wave_index, point_count, grid_cells, slab_rows):
    points = lax.iota(jnp.int32, point_count)
    along_x = points % grid_cells
    along_y = points // grid_cells % slab_rows
    along_z = points // (grid_cells * slab_rows)
    wave_x = wave_index // (grid_cells * grid_cells)
    wave_y = wave_index // grid_cells % grid_cells
    wave_z = wave_index % grid_cells
    phase_turns = (along_x[:, None] * wave_x[None, :] + along_y[:, None] * wave_y[None, :] + along_z[:, None] * wave_z[None, :]) % grid_cells
    angles = phase_turns.astype(jnp.float32) * (2.0 * math.pi / grid_cells)
    return jnp.concatenate([jnp.cos(angles), jnp.sin(angles)], axis=1).astype(jnp.bfloat16)

def reference(val_orbitals, cond_orbitals, val_energy, cond_energy, wave_index):
    row_table = phase_table(wave_index, NPTS, NG, SLAB_Y)
    window_table = phase_table(wave_index[:NW], NPTS, NG, SLAB_Y)
    cond_energies = cond_energy.astype(jnp.float32)
    cond_values = cond_orbitals.astype(jnp.float32)

    def one_valence(totals, inputs):
        orbital, energy = inputs
        density = (cond_values * orbital[None, :].astype(jnp.float32)).astype(jnp.bfloat16)
        window_terms = jnp.dot(density, window_table, preferred_element_type=jnp.float32)
        weights = 1.0 / (cond_energies - energy.astype(jnp.float32))
        weighted = window_terms * weights[:, None]
        update = jnp.dot(weighted.T, density.astype(jnp.float32), precision=lax.Precision.HIGHEST)
        return (totals + update, None)
    totals, unused = lax.scan(one_valence, jnp.zeros((2 * NW, NPTS), jnp.float32), (val_orbitals, val_energy))
    products = jnp.dot(totals, row_table.astype(jnp.float32), precision=lax.Precision.HIGHEST)
    factor = -4.0 / math.sqrt(NVAL * NCOND)
    real_part = factor * (products[:NW, :NPW] + products[NW:, NPW:])
    imag_part = factor * (products[:NW, NPW:] - products[NW:, :NPW])
    return (real_part, imag_part)
```

```python
import functools
import math

import jax
import jax.numpy as jnp
from jax import lax
from jax.experimental import pallas as pl
from jax.experimental.pallas import tpu as pltpu
from jax.sharding import PartitionSpec as P

NG = 96
NW = 128
SLAB_Y = 4
LANES = 128
VMEM_LIMIT = 24 * 1024 * 1024
MESH = pl.DeviceIdType.MESH


def modulo(value, period):
    return value - period * jnp.floor((value + 0.5) * (1.0 / period))


def cos_turns(turns):
    angle = (turns - NG / 2) * (math.pi / NG)
    square = angle * angle
    series = 1.0
    for order in (10, 8, 6, 4, 2):
        series = 1.0 - square * series * (1.0 / (order * (order + 1)))
    sine = angle * series
    return 2.0 * sine * sine - 1.0


def wave_parts(flat):
    wave_x = jnp.floor((flat + 0.5) * (1.0 / (NG * NG)))
    rest = flat - wave_x * (NG * NG)
    wave_y = jnp.floor((rest + 0.5) * (1.0 / NG))
    return wave_x, wave_y, rest - wave_y * NG


def point_parts(point):
    plane = jnp.floor((point + 0.5) * (1.0 / NG))
    along_z = jnp.floor((plane + 0.5) * (1.0 / SLAB_Y))
    return point - plane * NG, plane - along_z * SLAB_Y, along_z


def iota(shape, axis):
    return lax.broadcasted_iota(jnp.int32, shape, axis).astype(jnp.float32)


def factors(index, points):
    wave_x, wave_y, wave_z = wave_parts(index.astype(jnp.float32))
    planes = points // NG
    along_x = iota((NG, LANES), 0)
    plane = iota((planes, LANES), 0)
    along_z = jnp.floor((plane + 0.5) * (1.0 / SLAB_Y))
    along_y = plane - along_z * SLAB_Y
    turns_x = modulo(along_x * wave_x, NG)
    turns_yz = modulo(along_y * wave_y + along_z * wave_z, NG)
    quarter = 3 * NG // 4
    return (
        cos_turns(turns_x),
        cos_turns(modulo(turns_x + quarter, NG)),
        cos_turns(turns_yz),
        cos_turns(modulo(turns_yz + quarter, NG)),
    )


def split(value):
    high = value.astype(jnp.bfloat16)
    low = (value - high.astype(jnp.float32)).astype(jnp.bfloat16)
    return jnp.concatenate([high, low], axis=0)


def dot(left, right):
    return jnp.dot(left, right, preferred_element_type=jnp.float32)


def dot_t(left, right):
    return lax.dot_general(left, right, (((1,), (1,)), ((), ())), preferred_element_type=jnp.float32)


def flip(position, size):
    if size % 2:
        return position
    return position + 1 - 2 * lax.rem(position, 2)


def nearest(position, step, size):
    both = jnp.minimum(position, size - 1 - position)
    half = (step + 1) // 2
    near = position + half if step % 2 else position - half
    side = jnp.where(position < size - 1 - position, 1, -1)
    return jnp.where(step <= 2 * both, near, position + side * (step - both))


def kernel(
    nv, nc, group, slots,
    val, cond, val_energy, cond_energy, wave, out,
    gath_v, gath_c, gath_ve, gath_ce, own_wave, window, cos_rows, sin_rows, window_table, dens, weights, totals,
    recv_v, recv_ve, recv_c, recv_ce, recv_w, send, ready_c, ready_v, local,
):
    iv = lax.axis_index("val")
    ic = lax.axis_index("cond")
    vb, points = val.shape
    cb = cond.shape[0]
    rows = NW // nv
    planes = points // NG
    steps = nc // group
    mine = ic // group
    rank = flip(iv, nv)

    barrier = pltpu.get_barrier_semaphore()

    def each(first, last, body):
        def step(j, carry):
            body(j)
            return carry

        lax.fori_loop(first, last, step, 0)

    def greet(axis, peer):
        pl.semaphore_signal(barrier, inc=1, device_id={axis: peer}, device_id_type=MESH)

    each(ic + 1, nc, lambda j: greet("cond", j))
    each(rank + 1, nv, lambda j: greet("val", flip(j, nv)))

    wave_copy = pltpu.make_async_copy(wave, own_wave, local.at[0])
    own_copies = [
        pltpu.make_async_copy(cond, gath_c.at[ic], local.at[1]),
        pltpu.make_async_copy(val, gath_v.at[iv], local.at[2]),
        pltpu.make_async_copy(cond_energy, gath_ce.at[ic], local.at[3]),
        pltpu.make_async_copy(val_energy, gath_ve.at[iv], local.at[4]),
    ]
    wave_copy.start()
    for copy in own_copies:
        copy.start()

    def remote(axis, peer, src, dst, send_sem, recv_sem):
        return pltpu.make_async_remote_copy(
            src_ref=src, dst_ref=dst, send_sem=send_sem, recv_sem=recv_sem,
            device_id={axis: peer}, device_id_type=MESH,
        )

    def send_cond(peer):
        remote("cond", peer, cond, gath_c.at[ic], send.at[0], recv_c.at[mine]).start()
        remote("cond", peer, cond_energy, gath_ce.at[ic], send.at[1], recv_ce.at[mine]).start()

    def send_val(peer):
        remote("val", peer, val, gath_v.at[iv], send.at[2], recv_v).start()
        remote("val", peer, val_energy, gath_ve.at[iv], send.at[3], recv_ve).start()

    def wait_for(part, semaphore):
        pltpu.make_async_copy(part, part, semaphore).wait()

    @pl.when(ic + rank > 0)
    def _():
        pl.semaphore_wait(barrier, ic + rank)

    each(0, ic, lambda j: pl.semaphore_signal(
        ready_c.at[mine], inc=1, device_id={"cond": j}, device_id_type=MESH))
    each(0, rank, lambda j: pl.semaphore_signal(
        ready_v, inc=1, device_id={"val": flip(j, nv)}, device_id_type=MESH))
    each(0, ic, send_cond)
    each(0, rank, lambda j: send_val(flip(j, nv)))

    wave_copy.wait()
    for block in range(own_wave.shape[0]):
        cos_x, sin_x, cos_p, sin_p = factors(own_wave[pl.ds(block, 1), :], points)
        lanes = pl.ds(block * LANES, LANES)
        for plane in range(planes):
            at = pl.ds(plane * NG, NG)
            c, s = cos_p[plane:plane + 1, :], sin_p[plane:plane + 1, :]
            cos_rows[at, lanes] = (cos_x * c - sin_x * s).astype(jnp.bfloat16)
            sin_rows[at, lanes] = (sin_x * c + cos_x * s).astype(jnp.bfloat16)

    def window_to(peer):
        @pl.when(ic == 0)
        def _():
            remote("cond", peer, own_wave.at[pl.ds(0, 1)], window, send.at[4], recv_w).start()

    own_window = pltpu.make_async_copy(wave.at[pl.ds(0, 1)], window, local.at[0])

    @pl.when(ic == 0)
    def _():
        own_window.start()

    @pl.when(rank < nv - 1)
    def _():
        pl.semaphore_wait(ready_v, nv - 1 - rank)

    each(rank + 1, nv, lambda j: send_val(flip(j, nv)))

    if group == 2:
        @pl.when(lax.rem(ic, 2) == 0)
        def _():
            pl.semaphore_wait(ready_c.at[mine], 1)
            window_to(ic + 1)
            send_cond(ic + 1)

    def serve(step):
        other = nearest(mine, step, steps)

        @pl.when(other > mine)
        def _():
            pl.semaphore_wait(ready_c.at[other], group)
            for j in range(group):
                window_to(other * group + j)
            for j in range(group):
                send_cond(other * group + j)

    if steps > 1:
        serve(1)
    for copy in own_copies:
        copy.wait()
    wait_for(gath_v.at[pl.ds(0, nv - 1)], recv_v)
    wait_for(gath_ve.at[pl.ds(0, nv - 1)], recv_ve)

    count = group * cb
    height = nv * vb * count
    pair = iota((1, height), 1)
    pair_v = jnp.floor((pair + 0.5) * (1.0 / count))
    pair_c = pair - pair_v * count

    def spread(row, length, index, offset):
        square = jnp.broadcast_to(row.astype(jnp.float32), (length, length))
        eye = iota((length, length), 0) == iota((length, length), 1)
        column = jnp.sum(jnp.where(eye, square, 0.0), axis=1, keepdims=True)
        chosen = iota((length, height), 0) + offset == index
        return jnp.sum(jnp.where(chosen, column, 0.0), axis=0, keepdims=True)

    own_val = sum(spread(gath_ve[b], vb, pair_v, b * vb) for b in range(nv))

    def fill(step):
        slot = step % slots
        if step:
            other = nearest(mine, step, steps)
            wait_for(gath_c.at[pl.ds(other * group, group)], recv_c.at[other])
            wait_for(gath_ce.at[pl.ds(other * group, group)], recv_ce.at[other])
        else:
            other = mine
            if group == 2:
                wait_for(gath_c.at[flip(ic, nc)], recv_c.at[mine])
                wait_for(gath_ce.at[flip(ic, nc)], recv_ce.at[mine])
        at = [other * group + j for j in range(group)]
        orbitals = jnp.concatenate([gath_c[j] for j in at], axis=0)
        own_cond = sum(spread(gath_ce[j], cb, pair_c, n * cb) for n, j in enumerate(at))
        weights[0:1, slot * height:(slot + 1) * height] = 1.0 / (own_cond - own_val)

        def one_block(b, carry):
            block = gath_v[b]
            for v in range(vb):
                first = pl.multiple_of(slot * height + (b * vb + v) * count, count)
                dens[pl.ds(first, count), :] = orbitals * block[v:v + 1, :]
            return carry

        lax.fori_loop(0, nv, one_block, 0, unroll=nv <= 4)

    def use(step, span):
        slot = step % slots
        at = pl.ds(slot * height, span * height)
        weighted = dot_t(window_table[...], dens[at, :]) * weights[0:1, slot * height:(slot + span) * height]
        update = dot(split(weighted), dens[at, :])
        update = update[0:2 * rows] + update[2 * rows:4 * rows]
        totals[...] = update if step == 0 else totals[...] + update

    fill(0)
    for step in range(2, steps):
        serve(step)
    if steps > 1:
        fill(1)

    @pl.when(ic == 0)
    def _():
        own_window.wait()

    @pl.when(ic != 0)
    def _():
        wait_for(window, recv_w)

    spread_wave = jnp.broadcast_to(window[...], (8, LANES))
    first = pltpu.roll(spread_wave, lax.rem(NW - iv * rows, NW), 1)
    lane = lax.broadcasted_iota(jnp.int32, (8, LANES), 1)
    index = jnp.where(lane < rows, first, pltpu.roll(first, rows, 1))[0:1, :].astype(jnp.float32)
    index = jnp.transpose(jnp.broadcast_to(index, (LANES, LANES)))[0:2 * rows]
    wave_x, wave_y, wave_z = wave_parts(index)
    shift = jnp.where(iota((2 * rows, LANES), 0) < rows, 0.0, 3 * NG / 4)
    for block in range(points // LANES):
        along_x, along_y, along_z = point_parts(iota((1, LANES), 1) + block * LANES)
        turns = modulo(wave_x * along_x + wave_y * along_y + wave_z * along_z + shift, NG)
        window_table[:, pl.ds(block * LANES, LANES)] = cos_turns(turns).astype(jnp.bfloat16)

    begun = min(2, steps)
    use(0, begun)
    for step in range(begun, steps):
        fill(step)
        use(step, 1)

    sums = split(totals[...])
    by_cos = dot(sums, cos_rows[...])
    by_sin = dot(sums, sin_rows[...])
    by_cos = by_cos[0:2 * rows] + by_cos[2 * rows:4 * rows]
    by_sin = by_sin[0:2 * rows] + by_sin[2 * rows:4 * rows]
    out[0:rows, :] = by_cos[0:rows] + by_sin[rows:2 * rows]
    out[rows:2 * rows, :] = by_sin[0:rows] - by_cos[rows:2 * rows]

    wait_for(gath_c.at[pl.ds(0, nc - 1)], send.at[0])
    wait_for(gath_ce.at[pl.ds(0, nc - 1)], send.at[1])
    wait_for(gath_v.at[pl.ds(0, nv - 1)], send.at[2])
    wait_for(gath_ve.at[pl.ds(0, nv - 1)], send.at[3])

    @pl.when(ic == 0)
    def _():
        each(1, nc, lambda j: wait_for(window, send.at[4]))


def per_device(val_orbitals, cond_orbitals, val_energy, cond_energy, wave_index):
    nv, nc = lax.axis_size("val"), lax.axis_size("cond")
    vb, points = val_orbitals.shape
    cb = cond_orbitals.shape[0]
    count = wave_index.shape[0]
    rows = NW // nv
    group = 2 if nc % 2 == 0 else 1
    steps = nc // group
    slots = min(4, steps)
    height = nv * vb * group * cb
    bf16, f32 = jnp.bfloat16, jnp.float32
    dma = pltpu.SemaphoreType.DMA
    regular = pltpu.SemaphoreType.REGULAR
    out = pl.pallas_call(
        functools.partial(kernel, nv, nc, group, slots),
        out_shape=jax.ShapeDtypeStruct((2 * rows, count), f32),
        in_specs=[pl.BlockSpec(memory_space=pltpu.HBM)] * 5,
        out_specs=pl.BlockSpec(memory_space=pltpu.VMEM),
        scratch_shapes=[
            pltpu.VMEM((nv, vb, points), bf16),
            pltpu.VMEM((nc, cb, points), bf16),
            pltpu.VMEM((nv, 1, vb), bf16),
            pltpu.VMEM((nc, 1, cb), bf16),
            pltpu.VMEM((count // LANES, LANES), jnp.int32),
            pltpu.VMEM((1, LANES), jnp.int32),
            pltpu.VMEM((points, count), bf16),
            pltpu.VMEM((points, count), bf16),
            pltpu.VMEM((2 * rows, points), bf16),
            pltpu.VMEM((slots * height, points), bf16),
            pltpu.VMEM((8, slots * height), f32),
            pltpu.VMEM((2 * rows, points), f32),
            dma, dma, dma((steps,)), dma((steps,)), dma, dma((5,)), regular((steps,)), regular, dma((5,)),
        ],
        compiler_params=pltpu.CompilerParams(
            collective_id=0, has_side_effects=True, vmem_limit_bytes=VMEM_LIMIT
        ),
    )(*[
        pltpu.with_memory_space_constraint(value, pltpu.HBM)
        for value in (
            val_orbitals, cond_orbitals, val_energy.reshape(1, vb), cond_energy.reshape(1, cb),
            wave_index.reshape(count // LANES, LANES),
        )
    ])
    factor = -4.0 / math.sqrt(nv * vb * nc * cb)
    return factor * out[0:rows], factor * out[rows:2 * rows]


def solution(mesh):
    return jax.shard_map(
        per_device,
        mesh=mesh,
        in_specs=(P("val", None), P("cond", None), P("val"), P("cond"), P("cond")),
        out_specs=(P("val", "cond"), P("val", "cond")),
        check_vma=False,
    )
```

```python
import functools
import math

import jax
import jax.numpy as jnp
from jax import lax
from jax.experimental import pallas as pl
from jax.experimental.pallas import tpu as pltpu
from jax.sharding import PartitionSpec as P

NG = 96
NW = 128
SLAB_Y = 4
LANES = 128
VMEM_LIMIT = 24 * 1024 * 1024
MESH = pl.DeviceIdType.MESH


def modulo(value, period):
    return value - period * jnp.floor((value + 0.5) * (1.0 / period))


def cos_turns(turns):
    angle = (turns - NG / 2) * (math.pi / NG)
    square = angle * angle
    series = 1.0
    for order in (10, 8, 6, 4, 2):
        series = 1.0 - square * series * (1.0 / (order * (order + 1)))
    sine = angle * series
    return 2.0 * sine * sine - 1.0


def wave_parts(flat):
    wave_x = jnp.floor((flat + 0.5) * (1.0 / (NG * NG)))
    rest = flat - wave_x * (NG * NG)
    wave_y = jnp.floor((rest + 0.5) * (1.0 / NG))
    return wave_x, wave_y, rest - wave_y * NG


def point_parts(point):
    plane = jnp.floor((point + 0.5) * (1.0 / NG))
    along_z = jnp.floor((plane + 0.5) * (1.0 / SLAB_Y))
    return point - plane * NG, plane - along_z * SLAB_Y, along_z


def iota(shape, axis):
    return lax.broadcasted_iota(jnp.int32, shape, axis).astype(jnp.float32)


def factors(index, points):
    wave_x, wave_y, wave_z = wave_parts(index.astype(jnp.float32))
    planes = points // NG
    along_x = iota((NG, LANES), 0)
    plane = iota((planes, LANES), 0)
    along_z = jnp.floor((plane + 0.5) * (1.0 / SLAB_Y))
    along_y = plane - along_z * SLAB_Y
    turns_x = modulo(along_x * wave_x, NG)
    turns_yz = modulo(along_y * wave_y + along_z * wave_z, NG)
    quarter = 3 * NG // 4
    return (
        cos_turns(turns_x),
        cos_turns(modulo(turns_x + quarter, NG)),
        cos_turns(turns_yz),
        cos_turns(modulo(turns_yz + quarter, NG)),
    )


def split(value):
    high = value.astype(jnp.bfloat16)
    low = (value - high.astype(jnp.float32)).astype(jnp.bfloat16)
    return jnp.concatenate([high, low], axis=0)


def dot(left, right):
    return jnp.dot(left, right, preferred_element_type=jnp.float32)


def dot_t(left, right):
    return lax.dot_general(left, right, (((1,), (1,)), ((), ())), preferred_element_type=jnp.float32)


def flip(position, size):
    if size % 2:
        return position
    return position + 1 - 2 * lax.rem(position, 2)


def nearest(position, step, size):
    both = jnp.minimum(position, size - 1 - position)
    half = (step + 1) // 2
    near = position + half if step % 2 else position - half
    side = jnp.where(position < size - 1 - position, 1, -1)
    return jnp.where(step <= 2 * both, near, position + side * (step - both))


def kernel(
    nv, nc, slots,
    val, cond, val_energy, cond_energy, wave, out,
    gath_v, gath_c, gath_ve, gath_ce, own_wave, window, cos_rows, sin_rows, window_table, dens, weights, totals,
    recv_v, recv_ve, recv_c, recv_ce, recv_w, send, ready, local,
):
    iv = lax.axis_index("val")
    ic = lax.axis_index("cond")
    vb, points = val.shape
    cb = cond.shape[0]
    rows = NW // nv
    planes = points // NG
    steps = nc // 2
    mine = ic // 2
    core = lax.rem(iv, 2)
    hub = iv - core
    scout = hub + 1
    is_hub = core == 0
    is_scout = core == 1

    barrier = pltpu.get_barrier_semaphore()

    def each(first, last, body):
        def step(j, carry):
            body(j)
            return carry

        lax.fori_loop(first, last, step, 0)

    def signal(semaphore, v, c):
        pl.semaphore_signal(semaphore, inc=1, device_id={"val": v, "cond": c}, device_id_type=MESH)

    @pl.when(ic == 0)
    def _():
        each(1, nc, lambda j: signal(barrier, scout, nc - j))

    @pl.when(ic > 0)
    def _():
        each(ic + 1, nc, lambda j: signal(barrier, hub, j))

    @pl.when(is_scout)
    def _():
        signal(barrier, hub, ic)

    each(1, nv // 2, lambda k: signal(barrier, lax.rem(hub + 2 * k, nv), ic))

    wave_copy = pltpu.make_async_copy(wave, own_wave, local.at[0])
    own_copies = [
        pltpu.make_async_copy(cond, gath_c.at[ic], local.at[1]),
        pltpu.make_async_copy(val, gath_v.at[iv], local.at[2]),
        pltpu.make_async_copy(cond_energy, gath_ce.at[ic], local.at[3]),
        pltpu.make_async_copy(val_energy, gath_ve.at[iv], local.at[4]),
    ]
    wave_copy.start()
    for copy in own_copies:
        copy.start()

    def remote(v, c, src, dst, semaphore):
        pltpu.make_async_remote_copy(
            src_ref=src, dst_ref=dst, send_sem=send, recv_sem=semaphore,
            device_id={"val": v, "cond": c}, device_id_type=MESH,
        ).start()

    def send_cond(v, c):
        remote(v, c, cond, gath_c.at[ic], recv_c.at[mine])
        remote(v, c, cond_energy, gath_ce.at[ic], recv_ce.at[mine])

    def send_val():
        def one(k):
            peer = lax.rem(iv + k, nv)
            remote(peer, ic, val, gath_v.at[iv], recv_v)
            remote(peer, ic, val_energy, gath_ve.at[iv], recv_ve)

        each(1, nv, one)

    def send_origin(v, c, source, first, count):
        part, energies = gath_c.at[pl.ds(first, count)], gath_ce.at[pl.ds(first, count)]
        remote(v, c, source, window, recv_w)
        remote(v, c, part, part, recv_c.at[0])
        remote(v, c, energies, energies, recv_ce.at[0])

    def wait_for(part, semaphore):
        pltpu.make_async_copy(part, part, semaphore).wait()

    @pl.when(is_scout & (ic > 0))
    def _():
        pl.semaphore_wait(barrier, 2)
        signal(ready.at[ic], scout, 0)
        send_cond(hub, 0)
        send_cond(scout, 0)

    @pl.when(is_hub)
    def _():
        pl.semaphore_wait(barrier, nv - 1 + 2 * jnp.maximum(ic - 1, 0))
        signal(ready.at[ic], scout, ic)
        each(2, ic, lambda j: signal(ready.at[ic], hub, j))

        def both(j):
            send_cond(hub, j)
            send_cond(scout, j)

        each(1, ic, both)
        send_val()

    wave_copy.wait()
    for block in range(own_wave.shape[0]):
        cos_x, sin_x, cos_p, sin_p = factors(own_wave[pl.ds(block, 1), :], points)
        lanes = pl.ds(block * LANES, LANES)
        for plane in range(planes):
            at = pl.ds(plane * NG, NG)
            c, s = cos_p[plane:plane + 1, :], sin_p[plane:plane + 1, :]
            cos_rows[at, lanes] = (cos_x * c - sin_x * s).astype(jnp.bfloat16)
            sin_rows[at, lanes] = (sin_x * c + cos_x * s).astype(jnp.bfloat16)
    for copy in own_copies:
        copy.wait()

    @pl.when(is_scout)
    def _():
        pl.semaphore_wait(ready.at[ic], 1)
        send_val()

    def wait_origin(first, count):
        wait_for(gath_c.at[pl.ds(first, count)], recv_c.at[0])
        wait_for(gath_ce.at[pl.ds(first, count)], recv_ce.at[0])

    own_window = own_wave.at[pl.ds(0, 1)]

    @pl.when(is_scout & (ic == 0))
    def _():
        pl.semaphore_wait(ready.at[1], 1)
        send_origin(scout, 1, own_window, 0, 1)
        wait_origin(1, 1)

        def serve(j):
            pl.semaphore_wait(ready.at[j], 1)
            send_origin(scout, j, own_window, 0, 2)

        each(2, nc, serve)

    @pl.when(is_hub & (ic > 1))
    def _():
        def serve(j):
            pl.semaphore_wait(ready.at[j], 1)
            send_cond(hub, j)
            send_cond(scout, j)

        each(ic + 1, nc, serve)

    @pl.when(ic == 0)
    def _():
        copy = pltpu.make_async_copy(own_window, window, local.at[0])
        copy.start()
        copy.wait()

    @pl.when(is_hub & (ic == 0))
    def _():
        wait_origin(1, 1)

    @pl.when(ic > 0)
    def _():
        wait_for(window, recv_w)

    @pl.when(ic == 1)
    def _():
        wait_origin(0, 1)

    @pl.when(ic > 1)
    def _():
        wait_origin(0, 2)

    @pl.when(is_scout & (ic == 1))
    def _():
        send_origin(hub, ic, window, 0, 1)

    @pl.when(is_scout & (ic > 1))
    def _():
        send_origin(hub, ic, window, 0, 2)

    spread_wave = jnp.broadcast_to(window[...], (8, LANES))
    first = pltpu.roll(spread_wave, lax.rem(NW - iv * rows, NW), 1)
    lane = lax.broadcasted_iota(jnp.int32, (8, LANES), 1)
    index = jnp.where(lane < rows, first, pltpu.roll(first, rows, 1))[0:1, :].astype(jnp.float32)
    index = jnp.transpose(jnp.broadcast_to(index, (LANES, LANES)))[0:2 * rows]
    wave_x, wave_y, wave_z = wave_parts(index)
    shift = jnp.where(iota((2 * rows, LANES), 0) < rows, 0.0, 3 * NG / 4)
    for block in range(points // LANES):
        along_x, along_y, along_z = point_parts(iota((1, LANES), 1) + block * LANES)
        turns = modulo(wave_x * along_x + wave_y * along_y + wave_z * along_z + shift, NG)
        window_table[:, pl.ds(block * LANES, LANES)] = cos_turns(turns).astype(jnp.bfloat16)

    wait_for(gath_v.at[pl.ds(0, nv - 1)], recv_v)
    wait_for(gath_ve.at[pl.ds(0, nv - 1)], recv_ve)

    count = 2 * cb
    height = nv * vb * count
    pair = iota((1, height), 1)
    pair_v = jnp.floor((pair + 0.5) * (1.0 / count))
    pair_c = pair - pair_v * count

    def spread(row, length, index, offset):
        square = jnp.broadcast_to(row.astype(jnp.float32), (length, length))
        eye = iota((length, length), 0) == iota((length, length), 1)
        column = jnp.sum(jnp.where(eye, square, 0.0), axis=1, keepdims=True)
        chosen = iota((length, height), 0) + offset == index
        return jnp.sum(jnp.where(chosen, column, 0.0), axis=0, keepdims=True)

    own_val = sum(spread(gath_ve[b], vb, pair_v, b * vb) for b in range(nv))

    def fill(step):
        slot = step % slots
        if step == 0:
            other = mine
            peer = flip(ic, nc)

            @pl.when(mine > 0)
            def _():
                wait_for(gath_c.at[peer], recv_c.at[mine])
                wait_for(gath_ce.at[peer], recv_ce.at[mine])
        else:
            other = nearest(mine, step, steps)
            if step == 1:
                other = jnp.where(mine > 0, 0, other)
            else:
                other = jnp.where(mine > 0, nearest(mine - 1, step - 1, steps - 1) + 1, other)

            @pl.when(other > 0)
            def _():
                wait_for(gath_c.at[pl.ds(other * 2, 2)], recv_c.at[other])
                wait_for(gath_ce.at[pl.ds(other * 2, 2)], recv_ce.at[other])
        at = [other * 2, other * 2 + 1]
        orbitals = jnp.concatenate([gath_c[j] for j in at], axis=0)
        own_cond = sum(spread(gath_ce[j], cb, pair_c, n * cb) for n, j in enumerate(at))
        weights[0:1, slot * height:(slot + 1) * height] = 1.0 / (own_cond - own_val)

        def one_block(b, carry):
            block = gath_v[b]
            for v in range(vb):
                first = pl.multiple_of(slot * height + (b * vb + v) * count, count)
                dens[pl.ds(first, count), :] = orbitals * block[v:v + 1, :]
            return carry

        lax.fori_loop(0, nv, one_block, 0, unroll=nv <= 4)

    def use(step, span):
        slot = step % slots
        at = pl.ds(slot * height, span * height)
        weighted = dot_t(window_table[...], dens[at, :]) * weights[0:1, slot * height:(slot + span) * height]
        update = dot(split(weighted), dens[at, :])
        update = update[0:2 * rows] + update[2 * rows:4 * rows]
        totals[...] = update if step == 0 else totals[...] + update

    for step in range(0, steps, 2):
        span = min(2, steps - step)
        for n in range(span):
            fill(step + n)
        use(step, span)

    sums = split(totals[...])
    by_cos = dot(sums, cos_rows[...])
    by_sin = dot(sums, sin_rows[...])
    by_cos = by_cos[0:2 * rows] + by_cos[2 * rows:4 * rows]
    by_sin = by_sin[0:2 * rows] + by_sin[2 * rows:4 * rows]
    out[0:rows, :] = by_cos[0:rows] + by_sin[rows:2 * rows]
    out[rows:2 * rows, :] = by_sin[0:rows] - by_cos[rows:2 * rows]

    def sent(conds, windows):
        def one(j):
            wait_for(gath_c.at[0], send)
            wait_for(gath_ce.at[0], send)

        each(0, conds, one)
        each(0, windows, lambda j: wait_for(window, send))

    wait_for(gath_v.at[pl.ds(0, nv - 1)], send)
    wait_for(gath_ve.at[pl.ds(0, nv - 1)], send)

    @pl.when(is_hub & (ic > 1))
    def _():
        sent(2 * (nc - 2), 0)

    @pl.when(is_scout & (ic == 0))
    def _():
        sent(1 + 2 * (nc - 2), nc - 1)

    @pl.when(is_scout & (ic == 1))
    def _():
        sent(3, 1)

    @pl.when(is_scout & (ic > 1))
    def _():
        sent(4, 1)


def per_device(val_orbitals, cond_orbitals, val_energy, cond_energy, wave_index):
    nv, nc = lax.axis_size("val"), lax.axis_size("cond")
    vb, points = val_orbitals.shape
    cb = cond_orbitals.shape[0]
    count = wave_index.shape[0]
    rows = NW // nv
    steps = nc // 2
    slots = min(4, steps)
    height = nv * vb * 2 * cb
    bf16, f32 = jnp.bfloat16, jnp.float32
    dma = pltpu.SemaphoreType.DMA
    regular = pltpu.SemaphoreType.REGULAR
    out = pl.pallas_call(
        functools.partial(kernel, nv, nc, slots),
        out_shape=jax.ShapeDtypeStruct((2 * rows, count), f32),
        in_specs=[pl.BlockSpec(memory_space=pltpu.HBM)] * 5,
        out_specs=pl.BlockSpec(memory_space=pltpu.VMEM),
        scratch_shapes=[
            pltpu.VMEM((nv, vb, points), bf16),
            pltpu.VMEM((nc, cb, points), bf16),
            pltpu.VMEM((nv, 1, vb), bf16),
            pltpu.VMEM((nc, 1, cb), bf16),
            pltpu.VMEM((count // LANES, LANES), jnp.int32),
            pltpu.VMEM((1, LANES), jnp.int32),
            pltpu.VMEM((points, count), bf16),
            pltpu.VMEM((points, count), bf16),
            pltpu.VMEM((2 * rows, points), bf16),
            pltpu.VMEM((slots * height, points), bf16),
            pltpu.VMEM((8, slots * height), f32),
            pltpu.VMEM((2 * rows, points), f32),
            dma, dma, dma((steps,)), dma((steps,)), dma, dma, regular((nc,)), dma((5,)),
        ],
        compiler_params=pltpu.CompilerParams(
            collective_id=0, has_side_effects=True, vmem_limit_bytes=VMEM_LIMIT
        ),
    )(*[
        pltpu.with_memory_space_constraint(value, pltpu.HBM)
        for value in (
            val_orbitals, cond_orbitals, val_energy.reshape(1, vb), cond_energy.reshape(1, cb),
            wave_index.reshape(count // LANES, LANES),
        )
    ])
    factor = -4.0 / math.sqrt(nv * vb * nc * cb)
    return factor * out[0:rows], factor * out[rows:2 * rows]


def solution(mesh):
    return jax.shard_map(
        per_device,
        mesh=mesh,
        in_specs=(P("val", None), P("cond", None), P("val"), P("cond"), P("cond")),
        out_specs=(P("val", "cond"), P("val", "cond")),
        check_vma=False,
    )
```

```python
import functools
import math

import jax
import jax.numpy as jnp
from jax import lax
from jax.experimental import pallas as pl
from jax.experimental.pallas import tpu as pltpu
from jax.sharding import PartitionSpec as P

NG = 96
NW = 128
SLAB_Y = 4
LANES = 128
VMEM_LIMIT = 24 * 1024 * 1024
MESH = pl.DeviceIdType.MESH


def modulo(value, period):
    return value - period * jnp.floor((value + 0.5) * (1.0 / period))


def cos_turns(turns):
    angle = (turns - NG / 2) * (math.pi / NG)
    square = angle * angle
    series = 1.0
    for order in (10, 8, 6, 4, 2):
        series = 1.0 - square * series * (1.0 / (order * (order + 1)))
    sine = angle * series
    return 2.0 * sine * sine - 1.0


def wave_parts(flat):
    wave_x = jnp.floor((flat + 0.5) * (1.0 / (NG * NG)))
    rest = flat - wave_x * (NG * NG)
    wave_y = jnp.floor((rest + 0.5) * (1.0 / NG))
    return wave_x, wave_y, rest - wave_y * NG


def point_parts(point):
    plane = jnp.floor((point + 0.5) * (1.0 / NG))
    along_z = jnp.floor((plane + 0.5) * (1.0 / SLAB_Y))
    return point - plane * NG, plane - along_z * SLAB_Y, along_z


def iota(shape, axis):
    return lax.broadcasted_iota(jnp.int32, shape, axis).astype(jnp.float32)


def factors(index, points):
    wave_x, wave_y, wave_z = wave_parts(index.astype(jnp.float32))
    planes = points // NG
    along_x = iota((NG, LANES), 0)
    plane = iota((planes, LANES), 0)
    along_z = jnp.floor((plane + 0.5) * (1.0 / SLAB_Y))
    along_y = plane - along_z * SLAB_Y
    turns_x = modulo(along_x * wave_x, NG)
    turns_yz = modulo(along_y * wave_y + along_z * wave_z, NG)
    quarter = 3 * NG // 4
    return (
        cos_turns(turns_x),
        cos_turns(modulo(turns_x + quarter, NG)),
        cos_turns(turns_yz),
        cos_turns(modulo(turns_yz + quarter, NG)),
    )


def split(value):
    high = value.astype(jnp.bfloat16)
    low = (value - high.astype(jnp.float32)).astype(jnp.bfloat16)
    return jnp.concatenate([high, low], axis=0)


def dot(left, right):
    return jnp.dot(left, right, preferred_element_type=jnp.float32)


def dot_t(left, right):
    return lax.dot_general(left, right, (((1,), (1,)), ((), ())), preferred_element_type=jnp.float32)


def flip(position, size):
    if size % 2:
        return position
    return position + 1 - 2 * lax.rem(position, 2)


def nearest(position, step, size):
    both = jnp.minimum(position, size - 1 - position)
    half = (step + 1) // 2
    near = position + half if step % 2 else position - half
    side = jnp.where(position < size - 1 - position, 1, -1)
    return jnp.where(step <= 2 * both, near, position + side * (step - both))


def kernel(
    nv, nc, slots,
    val, cond, val_energy, cond_energy, wave, out,
    gath_v, gath_c, gath_ve, gath_ce, own_wave, window, cos_rows, sin_rows, window_table, dens, weights, totals,
    recv_v, recv_ve, recv_c, recv_ce, recv_w, send, ready, ready_v, local,
):
    iv = lax.axis_index("val")
    ic = lax.axis_index("cond")
    vb, points = val.shape
    cb = cond.shape[0]
    rows = NW // nv
    planes = points // NG
    steps = nc // 2
    mine = ic // 2
    core = lax.rem(iv, 2)
    hub = iv - core
    scout = hub + 1
    chip = iv // 2
    chips = nv // 2
    is_hub = core == 0
    is_scout = core == 1

    barrier = pltpu.get_barrier_semaphore()

    def each(first, last, body):
        def step(j, carry):
            body(j)
            return carry

        lax.fori_loop(first, last, step, 0)

    def signal(semaphore, v, c):
        pl.semaphore_signal(semaphore, inc=1, device_id={"val": v, "cond": c}, device_id_type=MESH)

    @pl.when(ic == 0)
    def _():
        each(1, nc, lambda j: signal(barrier, scout, nc - j))

    @pl.when(ic > 0)
    def _():
        each(ic + 1, nc, lambda j: signal(barrier, hub, j))

    @pl.when(is_scout)
    def _():
        signal(barrier, hub, ic)

    each(chip + 1, chips, lambda k: signal(barrier, 2 * k, ic))

    @pl.when(ic == 0)
    def _():
        each(chip + 1, chips, lambda k: signal(barrier, 2 * k + 1, ic))


    wave_copy = pltpu.make_async_copy(wave, own_wave, local)
    own_copies = [
        pltpu.make_async_copy(cond, gath_c.at[ic], recv_c.at[mine]),
        pltpu.make_async_copy(val, gath_v.at[iv], recv_v),
        pltpu.make_async_copy(cond_energy, gath_ce.at[ic], recv_ce.at[mine]),
        pltpu.make_async_copy(val_energy, gath_ve.at[iv], recv_ve),
    ]
    wave_copy.start()
    for copy in own_copies:
        copy.start()

    def remote(v, c, src, dst, semaphore):
        pltpu.make_async_remote_copy(
            src_ref=src, dst_ref=dst, send_sem=send, recv_sem=semaphore,
            device_id={"val": v, "cond": c}, device_id_type=MESH,
        ).start()

    def send_cond(v, c):
        remote(v, c, cond, gath_c.at[ic], recv_c.at[mine])
        remote(v, c, cond_energy, gath_ce.at[ic], recv_ce.at[mine])

    def send_val(peer):
        remote(peer, ic, val, gath_v.at[iv], recv_v)
        remote(peer, ic, val_energy, gath_ve.at[iv], recv_ve)

    def send_window(v, c, source):
        remote(v, c, source, window, recv_w)

    def send_origin(v, c, first, count):
        part, energies = gath_c.at[pl.ds(first, count)], gath_ce.at[pl.ds(first, count)]
        remote(v, c, part, part, recv_c.at[0])
        remote(v, c, energies, energies, recv_ce.at[0])

    def wait_for(part, semaphore):
        pltpu.make_async_copy(part, part, semaphore).wait()

    @pl.when(is_scout & (ic > 0))
    def _():
        pl.semaphore_wait(barrier, 2)
        signal(ready.at[ic], scout, 0)
        send_cond(hub, 0)
        send_cond(scout, 0)

    @pl.when(is_scout & (ic == 0) & (chip > 0))
    def _():
        pl.semaphore_wait(barrier, 2 * chip)
        each(0, hub, send_val)

    @pl.when(is_hub)
    def _():
        pl.semaphore_wait(barrier, 1 + 2 * chip + 2 * jnp.maximum(ic - 1, 0))
        signal(ready.at[ic], scout, ic)
        each(2, ic, lambda j: signal(ready.at[ic], hub, j))

        def both(j):
            send_cond(hub, j)
            send_cond(scout, j)

        each(0, hub, lambda v: signal(ready_v, v, ic))
        each(1, ic, both)
        send_val(scout)
        each(0, hub, send_val)

    wave_copy.wait()
    for block in range(own_wave.shape[0]):
        cos_x, sin_x, cos_p, sin_p = factors(own_wave[pl.ds(block, 1), :], points)
        lanes = pl.ds(block * LANES, LANES)
        for plane in range(planes):
            at = pl.ds(plane * NG, NG)
            c, s = cos_p[plane:plane + 1, :], sin_p[plane:plane + 1, :]
            cos_rows[at, lanes] = (cos_x * c - sin_x * s).astype(jnp.bfloat16)
            sin_rows[at, lanes] = (sin_x * c + cos_x * s).astype(jnp.bfloat16)

    def serve(j):
        pl.semaphore_wait(ready.at[j], 1)
        send_cond(hub, j)
        send_cond(scout, j)

    @pl.when(is_hub & (ic > 1) & (lax.rem(ic, 2) == 0))
    def _():
        serve(ic + 1)

    @pl.when(is_scout)
    def _():
        pl.semaphore_wait(ready.at[ic], 1)
        send_val(hub)

        @pl.when(ic > 0)
        def _():
            each(0, hub, send_val)


    @pl.when(chip < chips - 1)
    def _():
        pl.semaphore_wait(ready_v, chips - 1 - chip)
        each(scout + 1, nv, send_val)

    def wait_origin():
        wait_for(gath_c.at[pl.ds(0, 2)], recv_c.at[0])
        wait_for(gath_ce.at[pl.ds(0, 2)], recv_ce.at[0])

    own_window = own_wave.at[pl.ds(0, 1)]

    @pl.when(is_scout & (ic == 0))
    def _():
        pl.semaphore_wait(ready.at[1], 1)
        send_window(scout, 1, own_window)
        send_cond(scout, 1)
        wait_origin()

        def serve_window(j):
            pl.semaphore_wait(ready.at[j], 1)
            send_window(scout, j, own_window)

            @pl.when(j > 3)
            def _():
                send_origin(scout, j - 2, 0, 2)

        each(2, nc, serve_window)
        each(nc - 2, nc, lambda j: send_origin(scout, j, 0, 2))

    @pl.when(is_hub & (ic > 1))
    def _():
        each(ic + 2 - lax.rem(ic, 2), nc, serve)

    @pl.when(is_scout & (ic > 0))
    def _():
        wait_for(window, recv_w)
        send_window(hub, ic, window)

    wait_for(gath_v, recv_v)
    wait_for(gath_ve, recv_ve)

    count = 2 * cb
    height = nv * vb * count
    pair = iota((1, height), 1)
    pair_v = jnp.floor((pair + 0.5) * (1.0 / count))
    pair_c = pair - pair_v * count

    def spread(row, length, index, offset):
        square = jnp.broadcast_to(row.astype(jnp.float32), (length, length))
        eye = iota((length, length), 0) == iota((length, length), 1)
        column = jnp.sum(jnp.where(eye, square, 0.0), axis=1, keepdims=True)
        chosen = iota((length, height), 0) + offset == index
        return jnp.sum(jnp.where(chosen, column, 0.0), axis=0, keepdims=True)

    own_val = sum(spread(gath_ve[b], vb, pair_v, b * vb) for b in range(nv))

    def fill(step):
        slot = step % slots
        if step == 0:
            other = mine

            @pl.when(mine > 0)
            def _():
                wait_for(gath_c.at[pl.ds(mine * 2, 2)], recv_c.at[mine])
                wait_for(gath_ce.at[pl.ds(mine * 2, 2)], recv_ce.at[mine])
        else:
            other = nearest(mine, step, steps)
            if step == 1:
                other = jnp.where(mine > 0, 0, other)

                @pl.when(is_hub & (mine > 0))
                def _():
                    wait_origin()

            else:
                other = jnp.where(mine > 0, nearest(mine - 1, step - 1, steps - 1) + 1, other)

            @pl.when(other > 0)
            def _():
                wait_for(gath_c.at[pl.ds(other * 2, 2)], recv_c.at[other])
                wait_for(gath_ce.at[pl.ds(other * 2, 2)], recv_ce.at[other])
        at = [other * 2, other * 2 + 1]
        orbitals = jnp.concatenate([gath_c[j] for j in at], axis=0)
        own_cond = sum(spread(gath_ce[j], cb, pair_c, n * cb) for n, j in enumerate(at))
        weights[0:1, slot * height:(slot + 1) * height] = 1.0 / (own_cond - own_val)

        def one_block(b, carry):
            block = gath_v[b]
            for v in range(vb):
                first = pl.multiple_of(slot * height + (b * vb + v) * count, count)
                dens[pl.ds(first, count), :] = orbitals * block[v:v + 1, :]
            return carry

        lax.fori_loop(0, nv, one_block, 0, unroll=nv <= 4)

    def use(step, span):
        slot = step % slots
        at = pl.ds(slot * height, span * height)
        weighted = dot_t(window_table[...], dens[at, :]) * weights[0:1, slot * height:(slot + span) * height]
        update = dot(split(weighted), dens[at, :])
        update = update[0:2 * rows] + update[2 * rows:4 * rows]
        totals[...] = update if step == 0 else totals[...] + update

    @pl.when(mine > 0)
    def _():
        fill(0)

    @pl.when(is_scout & (mine > 0))
    def _():
        wait_origin()
        send_origin(hub, ic, 0, 2)

    @pl.when(ic == 0)
    def _():
        copy = pltpu.make_async_copy(own_window, window, local)
        copy.start()
        copy.wait()

    @pl.when(is_hub & (ic > 0))
    def _():
        wait_for(window, recv_w)

    spread_wave = jnp.broadcast_to(window[...], (8, LANES))
    first = pltpu.roll(spread_wave, lax.rem(NW - iv * rows, NW), 1)
    lane = lax.broadcasted_iota(jnp.int32, (8, LANES), 1)
    index = jnp.where(lane < rows, first, pltpu.roll(first, rows, 1))[0:1, :].astype(jnp.float32)
    index = jnp.transpose(jnp.broadcast_to(index, (LANES, LANES)))[0:2 * rows]
    wave_x, wave_y, wave_z = wave_parts(index)
    shift = jnp.where(iota((2 * rows, LANES), 0) < rows, 0.0, 3 * NG / 4)
    for block in range(points // LANES):
        along_x, along_y, along_z = point_parts(iota((1, LANES), 1) + block * LANES)
        turns = modulo(wave_x * along_x + wave_y * along_y + wave_z * along_z + shift, NG)
        window_table[:, pl.ds(block * LANES, LANES)] = cos_turns(turns).astype(jnp.bfloat16)
    @pl.when(is_hub & (ic == 0))
    def _():
        wait_origin()

    @pl.when(ic == 1)
    def _():
        wait_origin()

    @pl.when(is_scout & (ic == 1))
    def _():
        send_origin(hub, ic, 0, 1)


    @pl.when(mine == 0)
    def _():
        fill(0)

    def wait_sent():
        def sent(conds, windows):
            def one(j):
                wait_for(gath_c.at[0], send)
                wait_for(gath_ce.at[0], send)

            each(0, conds, one)
            each(0, windows, lambda j: wait_for(window, send))

        wait_for(gath_v.at[pl.ds(0, nv - 1)], send)
        wait_for(gath_ve.at[pl.ds(0, nv - 1)], send)

        @pl.when(is_hub & (ic > 1))
        def _():
            sent(2 * (nc - 2), 0)

        @pl.when(is_scout & (ic == 0))
        def _():
            sent(1 + 2 * (nc - 2), nc - 1)

        @pl.when(is_scout & (ic == 1))
        def _():
            sent(3, 1)

        @pl.when(is_scout & (ic > 1))
        def _():
            sent(4, 1)

    def stages(span):
        for step in range(0, steps, span):
            last = min(step + span, steps)
            if last == steps:
                wait_sent()
            order = list(range(max(step, 1), last))
            if span > 2 and step == 0 and last > 2:
                order[0:2] = [2, 1]
            for n in order:
                fill(n)
            use(step, last - step)

    late = is_hub & (mine > 0)

    @pl.when(late)
    def _():
        stages(4)

    @pl.when(jnp.logical_not(late))
    def _():
        stages(2)

    sums = split(totals[...])
    by_cos = dot(sums, cos_rows[...])
    by_sin = dot(sums, sin_rows[...])
    by_cos = by_cos[0:2 * rows] + by_cos[2 * rows:4 * rows]
    by_sin = by_sin[0:2 * rows] + by_sin[2 * rows:4 * rows]
    out[0:rows, :] = by_cos[0:rows] + by_sin[rows:2 * rows]
    out[rows:2 * rows, :] = by_sin[0:rows] - by_cos[rows:2 * rows]


def per_device(val_orbitals, cond_orbitals, val_energy, cond_energy, wave_index):
    nv, nc = lax.axis_size("val"), lax.axis_size("cond")
    vb, points = val_orbitals.shape
    cb = cond_orbitals.shape[0]
    count = wave_index.shape[0]
    rows = NW // nv
    steps = nc // 2
    slots = min(4, steps)
    height = nv * vb * 2 * cb
    bf16, f32 = jnp.bfloat16, jnp.float32
    dma = pltpu.SemaphoreType.DMA
    regular = pltpu.SemaphoreType.REGULAR
    out = pl.pallas_call(
        functools.partial(kernel, nv, nc, slots),
        out_shape=jax.ShapeDtypeStruct((2 * rows, count), f32),
        in_specs=[pl.BlockSpec(memory_space=pltpu.HBM)] * 5,
        out_specs=pl.BlockSpec(memory_space=pltpu.VMEM),
        scratch_shapes=[
            pltpu.VMEM((nv, vb, points), bf16),
            pltpu.VMEM((nc, cb, points), bf16),
            pltpu.VMEM((nv, 1, vb), bf16),
            pltpu.VMEM((nc, 1, cb), bf16),
            pltpu.VMEM((count // LANES, LANES), jnp.int32),
            pltpu.VMEM((1, LANES), jnp.int32),
            pltpu.VMEM((points, count), bf16),
            pltpu.VMEM((points, count), bf16),
            pltpu.VMEM((2 * rows, points), bf16),
            pltpu.VMEM((slots * height, points), bf16),
            pltpu.VMEM((8, slots * height), f32),
            pltpu.VMEM((2 * rows, points), f32),
            dma, dma, dma((steps,)), dma((steps,)), dma, dma, regular((nc,)), regular, dma,
        ],
        compiler_params=pltpu.CompilerParams(
            collective_id=0, has_side_effects=True, vmem_limit_bytes=VMEM_LIMIT
        ),
    )(*[
        pltpu.with_memory_space_constraint(value, pltpu.HBM)
        for value in (
            val_orbitals, cond_orbitals, val_energy.reshape(1, vb), cond_energy.reshape(1, cb),
            wave_index.reshape(count // LANES, LANES),
        )
    ])
    factor = -4.0 / math.sqrt(nv * vb * nc * cb)
    return factor * out[0:rows], factor * out[rows:2 * rows]


def solution(mesh):
    return jax.shard_map(
        per_device,
        mesh=mesh,
        in_specs=(P("val", None), P("cond", None), P("val"), P("cond"), P("cond")),
        out_specs=(P("val", "cond"), P("val", "cond")),
        check_vma=False,
    )
```

```python
import functools
import math

import jax
import jax.numpy as jnp
from jax import lax
from jax.experimental import pallas as pl
from jax.experimental.pallas import tpu as pltpu
from jax.sharding import PartitionSpec as P

NG = 96
NW = 128
SLAB_Y = 4
LANES = 128
VMEM_LIMIT = 24 * 1024 * 1024
MESH = pl.DeviceIdType.MESH


def modulo(value, period):
    return value - period * jnp.floor((value + 0.5) * (1.0 / period))


def cos_turns(turns):
    angle = (turns - NG / 2) * (math.pi / NG)
    square = angle * angle
    series = 1.0
    for order in (10, 8, 6, 4, 2):
        series = 1.0 - square * series * (1.0 / (order * (order + 1)))
    sine = angle * series
    return 2.0 * sine * sine - 1.0


def wave_parts(flat):
    wave_x = jnp.floor((flat + 0.5) * (1.0 / (NG * NG)))
    rest = flat - wave_x * (NG * NG)
    wave_y = jnp.floor((rest + 0.5) * (1.0 / NG))
    return wave_x, wave_y, rest - wave_y * NG


def point_parts(point):
    plane = jnp.floor((point + 0.5) * (1.0 / NG))
    along_z = jnp.floor((plane + 0.5) * (1.0 / SLAB_Y))
    return point - plane * NG, plane - along_z * SLAB_Y, along_z


def iota(shape, axis):
    return lax.broadcasted_iota(jnp.int32, shape, axis).astype(jnp.float32)


def factors(index, points):
    wave_x, wave_y, wave_z = wave_parts(index.astype(jnp.float32))
    planes = points // NG
    along_x = iota((NG, LANES), 0)
    plane = iota((planes, LANES), 0)
    along_z = jnp.floor((plane + 0.5) * (1.0 / SLAB_Y))
    along_y = plane - along_z * SLAB_Y
    turns_x = modulo(along_x * wave_x, NG)
    turns_yz = modulo(along_y * wave_y + along_z * wave_z, NG)
    quarter = 3 * NG // 4
    return (
        cos_turns(turns_x),
        cos_turns(modulo(turns_x + quarter, NG)),
        cos_turns(turns_yz),
        cos_turns(modulo(turns_yz + quarter, NG)),
    )


def split(value):
    high = value.astype(jnp.bfloat16)
    low = (value - high.astype(jnp.float32)).astype(jnp.bfloat16)
    return jnp.concatenate([high, low], axis=0)


def dot(left, right):
    return jnp.dot(left, right, preferred_element_type=jnp.float32)


def dot_t(left, right):
    return lax.dot_general(left, right, (((1,), (1,)), ((), ())), preferred_element_type=jnp.float32)


def flip(position, size):
    if size % 2:
        return position
    return position + 1 - 2 * lax.rem(position, 2)


def nearest(position, step, size):
    both = jnp.minimum(position, size - 1 - position)
    half = (step + 1) // 2
    near = position + half if step % 2 else position - half
    side = jnp.where(position < size - 1 - position, 1, -1)
    return jnp.where(step <= 2 * both, near, position + side * (step - both))


def kernel(
    nv, nc, slots,
    val, cond, val_energy, cond_energy, wave, out,
    gath_v, gath_c, gath_ve, gath_ce, own_wave, window, cos_rows, sin_rows, window_table, dens, weights, totals,
    recv_v, recv_ve, recv_c, recv_ce, recv_w, send, ready, ready_v, local,
):
    iv = lax.axis_index("val")
    ic = lax.axis_index("cond")
    vb, points = val.shape
    cb = cond.shape[0]
    rows = NW // nv
    planes = points // NG
    steps = nc // 2
    mine = ic // 2
    core = lax.rem(iv, 2)
    hub = iv - core
    scout = hub + 1
    chip = iv // 2
    chips = nv // 2
    is_hub = core == 0
    is_scout = core == 1

    barrier = pltpu.get_barrier_semaphore()

    def each(first, last, body):
        def step(j, carry):
            body(j)
            return carry

        lax.fori_loop(first, last, step, 0)

    def signal(semaphore, v, c):
        pl.semaphore_signal(semaphore, inc=1, device_id={"val": v, "cond": c}, device_id_type=MESH)

    @pl.when((ic == 0) & (is_scout | (chip == 0)))
    def _():
        each(1, nc, lambda j: signal(barrier, scout, nc - j))

    @pl.when(ic > 0)
    def _():
        each(ic + 1, nc, lambda j: signal(barrier, hub, j))

    @pl.when(is_scout)
    def _():
        signal(barrier, hub, ic)

    each(chip + 1, chips, lambda k: signal(barrier, 2 * k, ic))

    @pl.when(ic == 0)
    def _():
        each(chip + 1, chips, lambda k: signal(barrier, 2 * k + 1, ic))


    wave_copy = pltpu.make_async_copy(wave, own_wave, local)
    own_copies = [
        pltpu.make_async_copy(cond, gath_c.at[ic], recv_c.at[mine]),
        pltpu.make_async_copy(val, gath_v.at[iv], recv_v),
        pltpu.make_async_copy(cond_energy, gath_ce.at[ic], recv_ce.at[mine]),
        pltpu.make_async_copy(val_energy, gath_ve.at[iv], recv_ve),
    ]
    wave_copy.start()
    for copy in own_copies:
        copy.start()

    def remote(v, c, src, dst, semaphore):
        pltpu.make_async_remote_copy(
            src_ref=src, dst_ref=dst, send_sem=send, recv_sem=semaphore,
            device_id={"val": v, "cond": c}, device_id_type=MESH,
        ).start()

    def send_cond(v, c):
        remote(v, c, cond, gath_c.at[ic], recv_c.at[mine])
        remote(v, c, cond_energy, gath_ce.at[ic], recv_ce.at[mine])

    def send_val(peer):
        remote(peer, ic, val, gath_v.at[iv], recv_v)
        remote(peer, ic, val_energy, gath_ve.at[iv], recv_ve)

    def send_window(v, c, source):
        remote(v, c, source, window, recv_w)

    def send_origin(v, c, first, count):
        part, energies = gath_c.at[pl.ds(first, count)], gath_ce.at[pl.ds(first, count)]
        remote(v, c, part, part, recv_c.at[0])
        remote(v, c, energies, energies, recv_ce.at[0])

    def wait_for(part, semaphore):
        pltpu.make_async_copy(part, part, semaphore).wait()

    @pl.when(is_scout & (ic > 0))
    def _():
        pl.semaphore_wait(barrier, 2 - jnp.minimum(chip, 1))
        signal(ready.at[ic], scout, 0)

        @pl.when(chip == 0)
        def _():
            send_cond(hub, 0)

        send_cond(scout, 0)

    @pl.when(is_scout & (ic == 0) & (chip > 0))
    def _():
        pl.semaphore_wait(barrier, 2 * chip)
        each(0, hub, send_val)

    @pl.when(is_hub)
    def _():
        pl.semaphore_wait(barrier, 1 + 2 * chip + 2 * jnp.maximum(ic - 1, 0))
        signal(ready.at[ic], scout, ic)
        each(2, ic, lambda j: signal(ready.at[ic], hub, j))

        def both(j):
            send_cond(hub, j)
            send_cond(scout, j)

        each(0, hub, lambda v: signal(ready_v, v, ic))
        each(1, ic, both)
        send_val(scout)
        each(0, hub, send_val)

    wave_copy.wait()
    for block in range(own_wave.shape[0]):
        cos_x, sin_x, cos_p, sin_p = factors(own_wave[pl.ds(block, 1), :], points)
        lanes = pl.ds(block * LANES, LANES)
        for plane in range(planes):
            at = pl.ds(plane * NG, NG)
            c, s = cos_p[plane:plane + 1, :], sin_p[plane:plane + 1, :]
            cos_rows[at, lanes] = (cos_x * c - sin_x * s).astype(jnp.bfloat16)
            sin_rows[at, lanes] = (sin_x * c + cos_x * s).astype(jnp.bfloat16)

    own_window = own_wave.at[pl.ds(0, 1)]

    def make_window_table():
        spread_wave = jnp.broadcast_to(window[...], (8, LANES))
        first = pltpu.roll(spread_wave, lax.rem(NW - iv * rows, NW), 1)
        lane = lax.broadcasted_iota(jnp.int32, (8, LANES), 1)
        index = jnp.where(lane < rows, first, pltpu.roll(first, rows, 1))[0:1, :].astype(jnp.float32)
        index = jnp.transpose(jnp.broadcast_to(index, (LANES, LANES)))[0:2 * rows]
        wave_x, wave_y, wave_z = wave_parts(index)
        shift = jnp.where(iota((2 * rows, LANES), 0) < rows, 0.0, 3 * NG / 4)
        for block in range(points // LANES):
            along_x, along_y, along_z = point_parts(iota((1, LANES), 1) + block * LANES)
            turns = modulo(wave_x * along_x + wave_y * along_y + wave_z * along_z + shift, NG)
            window_table[:, pl.ds(block * LANES, LANES)] = cos_turns(turns).astype(jnp.bfloat16)

    @pl.when(ic == 0)
    def _():
        copy = pltpu.make_async_copy(own_window, window, local)
        copy.start()
        copy.wait()
        make_window_table()

    def serve(j):
        pl.semaphore_wait(ready.at[j], 1)
        send_cond(hub, j)
        send_cond(scout, j)

    @pl.when(is_hub & (ic > 1) & (lax.rem(ic, 2) == 0))
    def _():
        serve(ic + 1)

    @pl.when(is_scout)
    def _():
        pl.semaphore_wait(ready.at[ic], 1)
        send_val(hub)

        @pl.when(ic > 0)
        def _():
            each(0, hub, send_val)


    @pl.when(chip < chips - 1)
    def _():
        pl.semaphore_wait(ready_v, chips - 1 - chip)
        each(scout + 1, nv, send_val)

    def wait_origin():
        wait_for(gath_c.at[pl.ds(0, 2)], recv_c.at[0])
        wait_for(gath_ce.at[pl.ds(0, 2)], recv_ce.at[0])

    @pl.when(is_scout & (ic == 0))
    def _():
        pl.semaphore_wait(ready.at[1], 1)
        send_window(scout, 1, own_window)
        send_cond(scout, 1)
        wait_origin()

        @pl.when(chip > 0)
        def _():
            send_origin(hub, 0, 1, 1)

        def serve_window(j):
            pl.semaphore_wait(ready.at[j], 1)
            send_window(scout, j, own_window)

        def serve_pair(k):
            serve_window(2 * k)
            serve_window(2 * k + 1)
            send_origin(scout, 2 * k, 0, 2)
            send_origin(scout, 2 * k + 1, 0, 2)

        each(1, steps, serve_pair)

    @pl.when(is_hub & (ic > 1))
    def _():
        each(ic + 2 - lax.rem(ic, 2), nc, serve)

    @pl.when(is_scout & (ic > 0))
    def _():
        wait_for(window, recv_w)
        send_window(hub, ic, window)
        make_window_table()

    wait_for(gath_v, recv_v)
    wait_for(gath_ve, recv_ve)

    count = 2 * cb
    height = nv * vb * count
    pair = iota((1, height), 1)
    pair_v = jnp.floor((pair + 0.5) * (1.0 / count))
    pair_c = pair - pair_v * count

    def spread(row, length, index, offset):
        square = jnp.broadcast_to(row.astype(jnp.float32), (length, length))
        eye = iota((length, length), 0) == iota((length, length), 1)
        column = jnp.sum(jnp.where(eye, square, 0.0), axis=1, keepdims=True)
        chosen = iota((length, height), 0) + offset == index
        return jnp.sum(jnp.where(chosen, column, 0.0), axis=0, keepdims=True)

    own_val = sum(spread(gath_ve[b], vb, pair_v, b * vb) for b in range(nv))

    def fill(step):
        slot = step % slots
        if step == 0:
            other = mine

            @pl.when(mine > 0)
            def _():
                wait_for(gath_c.at[pl.ds(mine * 2, 2)], recv_c.at[mine])
                wait_for(gath_ce.at[pl.ds(mine * 2, 2)], recv_ce.at[mine])
        else:
            other = nearest(mine, step, steps)
            if step == 1:
                other = jnp.where(mine > 0, 0, other)

                @pl.when(is_hub & (mine > 0))
                def _():
                    wait_origin()

            else:
                other = jnp.where(mine > 0, nearest(mine - 1, step - 1, steps - 1) + 1, other)

            @pl.when(other > 0)
            def _():
                wait_for(gath_c.at[pl.ds(other * 2, 2)], recv_c.at[other])
                wait_for(gath_ce.at[pl.ds(other * 2, 2)], recv_ce.at[other])

            @pl.when(is_scout & (ic == 0) & (chip > 0))
            def _():
                part, energies = gath_c.at[pl.ds(other * 2, 2)], gath_ce.at[pl.ds(other * 2, 2)]
                remote(hub, ic, part, part, recv_c.at[other])
                remote(hub, ic, energies, energies, recv_ce.at[other])

        at = [other * 2, other * 2 + 1]
        orbitals = jnp.concatenate([gath_c[j] for j in at], axis=0)
        own_cond = sum(spread(gath_ce[j], cb, pair_c, n * cb) for n, j in enumerate(at))
        weights[0:1, slot * height:(slot + 1) * height] = 1.0 / (own_cond - own_val)

        def one_block(b, carry):
            block = gath_v[b]
            for v in range(vb):
                first = pl.multiple_of(slot * height + (b * vb + v) * count, count)
                dens[pl.ds(first, count), :] = orbitals * block[v:v + 1, :]
            return carry

        lax.fori_loop(0, nv, one_block, 0, unroll=nv <= 4)

    def use(step, span):
        slot = step % slots
        at = pl.ds(slot * height, span * height)
        weighted = dot_t(window_table[...], dens[at, :]) * weights[0:1, slot * height:(slot + span) * height]
        update = dot(split(weighted), dens[at, :])
        update = update[0:2 * rows] + update[2 * rows:4 * rows]
        update = update if step == 0 else totals[...] + update
        if step + span < steps:
            totals[...] = update
            return
        sums = split(update)
        by_cos = dot(sums, cos_rows[...])
        by_sin = dot(sums, sin_rows[...])
        by_cos = by_cos[0:2 * rows] + by_cos[2 * rows:4 * rows]
        by_sin = by_sin[0:2 * rows] + by_sin[2 * rows:4 * rows]
        out[0:rows, :] = by_cos[0:rows] + by_sin[rows:2 * rows]
        out[rows:2 * rows, :] = by_sin[0:rows] - by_cos[rows:2 * rows]

    @pl.when(mine > 0)
    def _():
        fill(0)

    @pl.when(is_scout & (mine > 0))
    def _():
        wait_origin()
        send_origin(hub, ic, 0, 2)

    @pl.when(is_hub & (ic > 0))
    def _():
        wait_for(window, recv_w)
        make_window_table()

    @pl.when(is_hub & (ic == 0))
    def _():
        wait_origin()

    @pl.when(ic == 1)
    def _():
        wait_origin()

    @pl.when(is_scout & (ic == 1))
    def _():
        send_origin(hub, ic, 0, 1)


    @pl.when(mine == 0)
    def _():
        fill(0)

    def sent(conds, windows):
        def one(j):
            wait_for(gath_c.at[0], send)
            wait_for(gath_ce.at[0], send)

        each(0, conds, one)
        each(0, windows, lambda j: wait_for(window, send))

    def wait_sent():
        wait_for(gath_v.at[pl.ds(0, nv - 1)], send)
        wait_for(gath_ve.at[pl.ds(0, nv - 1)], send)

        @pl.when(is_hub & (ic > 1))
        def _():
            sent(2 * (nc - 2), 0)

        @pl.when(is_scout & (ic == 1))
        def _():
            sent(3 - jnp.minimum(chip, 1), 1)

        @pl.when(is_scout & (ic > 1))
        def _():
            sent(4 - jnp.minimum(chip, 1), 1)

    def stages(ends):
        ends = [end for end in ends if end < steps] + list(range(slots, steps + 1, slots))
        step = 0
        for end in sorted(set(ends + [steps])):
            if end == steps:
                wait_sent()
            order = list(range(max(step, 1), end))
            if step == 0 and end > 2:
                order[0:2] = [2, 1]
            for n in order:
                fill(n)
            use(step, end - step)
            step = end

    late = is_hub & (mine > 0)

    @pl.when(late)
    def _():
        stages([3])

    @pl.when(jnp.logical_not(late))
    def _():
        stages([2])


    @pl.when(is_scout & (ic == 0))
    def _():
        sent(1 + 2 * (nc - 2) + (nc - 1) * jnp.minimum(chip, 1), nc - 1)


def per_device(val_orbitals, cond_orbitals, val_energy, cond_energy, wave_index):
    nv, nc = lax.axis_size("val"), lax.axis_size("cond")
    vb, points = val_orbitals.shape
    cb = cond_orbitals.shape[0]
    count = wave_index.shape[0]
    rows = NW // nv
    steps = nc // 2
    slots = min(4, steps)
    height = nv * vb * 2 * cb
    bf16, f32 = jnp.bfloat16, jnp.float32
    dma = pltpu.SemaphoreType.DMA
    regular = pltpu.SemaphoreType.REGULAR
    out = pl.pallas_call(
        functools.partial(kernel, nv, nc, slots),
        out_shape=jax.ShapeDtypeStruct((2 * rows, count), f32),
        in_specs=[pl.BlockSpec(memory_space=pltpu.HBM)] * 5,
        out_specs=pl.BlockSpec(memory_space=pltpu.VMEM),
        scratch_shapes=[
            pltpu.VMEM((nv, vb, points), bf16),
            pltpu.VMEM((nc, cb, points), bf16),
            pltpu.VMEM((nv, 1, vb), bf16),
            pltpu.VMEM((nc, 1, cb), bf16),
            pltpu.VMEM((count // LANES, LANES), jnp.int32),
            pltpu.VMEM((1, LANES), jnp.int32),
            pltpu.VMEM((points, count), bf16),
            pltpu.VMEM((points, count), bf16),
            pltpu.VMEM((2 * rows, points), bf16),
            pltpu.VMEM((slots * height, points), bf16),
            pltpu.VMEM((8, slots * height), f32),
            pltpu.VMEM((2 * rows, points), f32),
            dma, dma, dma((steps,)), dma((steps,)), dma, dma, regular((nc,)), regular, dma,
        ],
        compiler_params=pltpu.CompilerParams(
            collective_id=0, has_side_effects=True, vmem_limit_bytes=VMEM_LIMIT
        ),
    )(*[
        pltpu.with_memory_space_constraint(value, pltpu.HBM)
        for value in (
            val_orbitals, cond_orbitals, val_energy.reshape(1, vb), cond_energy.reshape(1, cb),
            wave_index.reshape(count // LANES, LANES),
        )
    ])
    factor = -4.0 / math.sqrt(nv * vb * nc * cb)
    return factor * out[0:rows], factor * out[rows:2 * rows]


def solution(mesh):
    return jax.shard_map(
        per_device,
        mesh=mesh,
        in_specs=(P("val", None), P("cond", None), P("val"), P("cond"), P("cond")),
        out_specs=(P("val", "cond"), P("val", "cond")),
        check_vma=False,
    )
```

```python
import functools
import math

import jax
import jax.numpy as jnp
from jax import lax
from jax.experimental import pallas as pl
from jax.experimental.pallas import tpu as pltpu
from jax.sharding import PartitionSpec as P

NG = 96
NW = 128
SLAB_Y = 4
LANES = 128
VMEM_LIMIT = 24 * 1024 * 1024
MESH = pl.DeviceIdType.MESH


def modulo(value, period):
    return value - period * jnp.floor((value + 0.5) * (1.0 / period))


def cos_turns(turns):
    angle = (turns - NG / 2) * (math.pi / NG)
    square = angle * angle
    series = 1.0
    for order in (10, 8, 6, 4, 2):
        series = 1.0 - square * series * (1.0 / (order * (order + 1)))
    sine = angle * series
    return 2.0 * sine * sine - 1.0


def wave_parts(flat):
    wave_x = jnp.floor((flat + 0.5) * (1.0 / (NG * NG)))
    rest = flat - wave_x * (NG * NG)
    wave_y = jnp.floor((rest + 0.5) * (1.0 / NG))
    return wave_x, wave_y, rest - wave_y * NG


def point_parts(point):
    plane = jnp.floor((point + 0.5) * (1.0 / NG))
    along_z = jnp.floor((plane + 0.5) * (1.0 / SLAB_Y))
    return point - plane * NG, plane - along_z * SLAB_Y, along_z


def iota(shape, axis):
    return lax.broadcasted_iota(jnp.int32, shape, axis).astype(jnp.float32)


def factors(index, points):
    wave_x, wave_y, wave_z = wave_parts(index.astype(jnp.float32))
    planes = points // NG
    along_x = iota((NG, LANES), 0)
    plane = iota((planes, LANES), 0)
    along_z = jnp.floor((plane + 0.5) * (1.0 / SLAB_Y))
    along_y = plane - along_z * SLAB_Y
    turns_x = modulo(along_x * wave_x, NG)
    turns_yz = modulo(along_y * wave_y + along_z * wave_z, NG)
    quarter = 3 * NG // 4
    return (
        cos_turns(turns_x),
        cos_turns(modulo(turns_x + quarter, NG)),
        cos_turns(turns_yz),
        cos_turns(modulo(turns_yz + quarter, NG)),
    )


def split(value):
    high = value.astype(jnp.bfloat16)
    low = (value - high.astype(jnp.float32)).astype(jnp.bfloat16)
    return jnp.concatenate([high, low], axis=0)


def dot(left, right):
    return jnp.dot(left, right, preferred_element_type=jnp.float32)


def dot_t(left, right):
    return lax.dot_general(left, right, (((1,), (1,)), ((), ())), preferred_element_type=jnp.float32)


def flip(position, size):
    if size % 2:
        return position
    return position + 1 - 2 * lax.rem(position, 2)


def nearest(position, step, size):
    both = jnp.minimum(position, size - 1 - position)
    half = (step + 1) // 2
    near = position + half if step % 2 else position - half
    side = jnp.where(position < size - 1 - position, 1, -1)
    return jnp.where(step <= 2 * both, near, position + side * (step - both))


def kernel(
    nv, nc, slots,
    val, cond, val_energy, cond_energy, wave, out,
    gath_v, gath_c, gath_ve, gath_ce, own_wave, window, cos_rows, sin_rows, window_table, dens, weights, totals,
    recv_v, recv_ve, recv_c, recv_ce, recv_w, send, ready, ready_v, local,
):
    iv = lax.axis_index("val")
    ic = lax.axis_index("cond")
    vb, points = val.shape
    cb = cond.shape[0]
    rows = NW // nv
    planes = points // NG
    steps = nc // 2
    mine = ic // 2
    core = lax.rem(iv, 2)
    hub = iv - core
    scout = hub + 1
    chip = iv // 2
    chips = nv // 2
    is_hub = core == 0
    is_scout = core == 1
    pairs = is_scout & (ic > 1) & (lax.rem(ic, 2) == 0)

    barrier = pltpu.get_barrier_semaphore()

    def each(first, last, body):
        def step(j, carry):
            body(j)
            return carry

        lax.fori_loop(first, last, step, 0)

    def signal(semaphore, v, c):
        pl.semaphore_signal(semaphore, inc=1, device_id={"val": v, "cond": c}, device_id_type=MESH)

    @pl.when((ic == 0) & (is_scout | (chip == 0)))
    def _():
        each(1, nc, lambda j: signal(barrier, scout, nc - j))

    @pl.when(is_scout & (ic > 0))
    def _():
        each(ic + 1, nc, lambda j: signal(barrier, hub, j))

    @pl.when(is_scout)
    def _():
        signal(barrier, hub, ic)

    each(chip + 1, chips, lambda k: signal(barrier, 2 * k, ic))

    @pl.when(ic == 0)
    def _():
        each(chip + 1, chips, lambda k: signal(barrier, 2 * k + 1, ic))


    wave_copy = pltpu.make_async_copy(wave, own_wave, local)
    own_copies = [
        pltpu.make_async_copy(cond, gath_c.at[ic], recv_c.at[mine]),
        pltpu.make_async_copy(val, gath_v.at[iv], recv_v),
        pltpu.make_async_copy(cond_energy, gath_ce.at[ic], recv_ce.at[mine]),
        pltpu.make_async_copy(val_energy, gath_ve.at[iv], recv_ve),
    ]
    wave_copy.start()
    for copy in own_copies:
        copy.start()

    def remote(v, c, src, dst, semaphore, late=0):
        pltpu.make_async_remote_copy(
            src_ref=src, dst_ref=dst, send_sem=send.at[late], recv_sem=semaphore,
            device_id={"val": v, "cond": c}, device_id_type=MESH,
        ).start()

    def send_cond(v, c):
        remote(v, c, cond, gath_c.at[ic], recv_c.at[mine])
        remote(v, c, cond_energy, gath_ce.at[ic], recv_ce.at[mine])

    def send_val(peer):
        remote(peer, ic, val, gath_v.at[iv], recv_v)
        remote(peer, ic, val_energy, gath_ve.at[iv], recv_ve)

    def send_window(v, c, source):
        remote(v, c, source, window, recv_w)

    def send_origin(v, c, first, count):
        part, energies = gath_c.at[pl.ds(first, count)], gath_ce.at[pl.ds(first, count)]
        remote(v, c, part, part, recv_c.at[0])
        remote(v, c, energies, energies, recv_ce.at[0])

    def wait_for(part, semaphore):
        pltpu.make_async_copy(part, part, semaphore).wait()

    @pl.when(is_scout & (ic > 0))
    def _():
        pl.semaphore_wait(barrier, 2 - jnp.minimum(chip, 1))
        signal(ready.at[ic], scout, 0)

        @pl.when(chip == 0)
        def _():
            send_cond(hub, 0)

        send_cond(scout, 0)

    @pl.when(is_scout & (ic == 0) & (chip > 0))
    def _():
        pl.semaphore_wait(barrier, 2 * chip)
        each(0, hub, send_val)

    @pl.when(is_hub)
    def _():
        pl.semaphore_wait(barrier, 1 + 2 * chip + jnp.maximum(ic - 1, 0))
        signal(ready.at[ic], scout, ic)
        each(2, ic, lambda j: signal(ready.at[ic], scout, j))

        each(0, hub, lambda v: signal(ready_v, v, ic))
        each(1, ic, lambda j: send_cond(scout, j))
        send_val(scout)
        each(0, hub, send_val)

    wave_copy.wait()
    for block in range(own_wave.shape[0]):
        cos_x, sin_x, cos_p, sin_p = factors(own_wave[pl.ds(block, 1), :], points)
        lanes = pl.ds(block * LANES, LANES)
        for plane in range(planes):
            at = pl.ds(plane * NG, NG)
            c, s = cos_p[plane:plane + 1, :], sin_p[plane:plane + 1, :]
            cos_rows[at, lanes] = (cos_x * c - sin_x * s).astype(jnp.bfloat16)
            sin_rows[at, lanes] = (sin_x * c + cos_x * s).astype(jnp.bfloat16)

    own_window = own_wave.at[pl.ds(0, 1)]

    def make_window_table():
        spread_wave = jnp.broadcast_to(window[...], (8, LANES))
        first = pltpu.roll(spread_wave, lax.rem(NW - iv * rows, NW), 1)
        lane = lax.broadcasted_iota(jnp.int32, (8, LANES), 1)
        index = jnp.where(lane < rows, first, pltpu.roll(first, rows, 1))[0:1, :].astype(jnp.float32)
        index = jnp.transpose(jnp.broadcast_to(index, (LANES, LANES)))[0:2 * rows]
        wave_x, wave_y, wave_z = wave_parts(index)
        shift = jnp.where(iota((2 * rows, LANES), 0) < rows, 0.0, 3 * NG / 4)
        for block in range(points // LANES):
            along_x, along_y, along_z = point_parts(iota((1, LANES), 1) + block * LANES)
            turns = modulo(wave_x * along_x + wave_y * along_y + wave_z * along_z + shift, NG)
            window_table[:, pl.ds(block * LANES, LANES)] = cos_turns(turns).astype(jnp.bfloat16)

    @pl.when(ic == 0)
    def _():
        copy = pltpu.make_async_copy(own_window, window, local)
        copy.start()
        copy.wait()
        make_window_table()

    def serve(j):
        pl.semaphore_wait(ready.at[j], 1)
        send_cond(hub, j)
        send_cond(scout, j)

    @pl.when(is_scout)
    def _():
        pl.semaphore_wait(ready.at[ic], 1)
        send_val(hub)

        @pl.when(ic > 0)
        def _():
            each(0, hub, send_val)

        @pl.when(pairs)
        def _():
            serve(ic + 1)

    @pl.when(chip < chips - 1)
    def _():
        pl.semaphore_wait(ready_v, chips - 1 - chip)
        each(scout + 1, nv, send_val)

    def wait_group(g):
        wait_for(gath_c.at[pl.ds(2 * g, 2)], recv_c.at[g])
        wait_for(gath_ce.at[pl.ds(2 * g, 2)], recv_ce.at[g])

    def wait_origin():
        wait_group(0)

    @pl.when(is_scout & (ic == 0))
    def _():
        pl.semaphore_wait(ready.at[1], 1)
        send_window(scout, 1, own_window)
        send_cond(scout, 1)
        wait_origin()

        @pl.when(chip > 0)
        def _():
            send_origin(hub, 0, 1, 1)

        def serve_window(j):
            pl.semaphore_wait(ready.at[j], 1)
            send_window(scout, j, own_window)

        def send_pair(k):
            send_origin(scout, 2 * k, 0, 2)
            send_origin(scout, 2 * k + 1, 0, 2)

        def serve_pair(k):
            serve_window(2 * k)

            @pl.when(k > 1)
            def _():
                send_pair(k - 1)

            serve_window(2 * k + 1)

        each(1, steps, serve_pair)
        send_pair(steps - 1)

    @pl.when(is_scout & (ic > 1))
    def _():
        def serve_both(k):
            serve(2 * k + 1)
            serve(2 * k)

        each(mine + 1, steps, serve_both)

    @pl.when(pairs)
    def _():
        wait_group(mine)
        part, energies = gath_c.at[ic + 1], gath_ce.at[ic + 1]
        remote(hub, ic, part, part, recv_c.at[mine])
        remote(hub, ic, energies, energies, recv_ce.at[mine])

    @pl.when(is_scout & (ic > 0))
    def _():
        wait_for(window, recv_w)
        send_window(hub, ic, window)
        make_window_table()

    wait_for(gath_v, recv_v)
    wait_for(gath_ve, recv_ve)

    count = 2 * cb
    height = nv * vb * count
    pair = iota((1, height), 1)
    pair_v = jnp.floor((pair + 0.5) * (1.0 / count))
    pair_c = pair - pair_v * count

    def spread(row, length, index, offset):
        square = jnp.broadcast_to(row.astype(jnp.float32), (length, length))
        eye = iota((length, length), 0) == iota((length, length), 1)
        column = jnp.sum(jnp.where(eye, square, 0.0), axis=1, keepdims=True)
        chosen = iota((length, height), 0) + offset == index
        return jnp.sum(jnp.where(chosen, column, 0.0), axis=0, keepdims=True)

    own_val = sum(spread(gath_ve[b], vb, pair_v, b * vb) for b in range(nv))

    def fill(step):
        slot = step % slots
        if step == 0:
            other = mine

            @pl.when((mine > 0) & jnp.logical_not(pairs))
            def _():
                wait_group(mine)
        else:
            other = nearest(mine, step, steps)
            if step == 1:
                other = jnp.where(mine > 0, 0, other)

                @pl.when(is_hub & (mine > 0))
                def _():
                    wait_origin()

            else:
                other = jnp.where(mine > 0, nearest(mine - 1, step - 1, steps - 1) + 1, other)

            @pl.when(other > 0)
            def _():
                wait_group(other)

            @pl.when(is_scout & (other > mine) & (ic + chip > 0))
            def _():
                part, energies = gath_c.at[pl.ds(other * 2, 2)], gath_ce.at[pl.ds(other * 2, 2)]
                remote(hub, ic, part, part, recv_c.at[other], 1)
                remote(hub, ic, energies, energies, recv_ce.at[other], 1)

        at = [other * 2, other * 2 + 1]
        orbitals = jnp.concatenate([gath_c[j] for j in at], axis=0)
        own_cond = sum(spread(gath_ce[j], cb, pair_c, n * cb) for n, j in enumerate(at))
        weights[0:1, slot * height:(slot + 1) * height] = 1.0 / (own_cond - own_val)

        def one_block(b, carry):
            block = gath_v[b]
            for v in range(vb):
                first = pl.multiple_of(slot * height + (b * vb + v) * count, count)
                dens[pl.ds(first, count), :] = orbitals * block[v:v + 1, :]
            return carry

        lax.fori_loop(0, nv, one_block, 0, unroll=nv <= 4)

    def use(step, span):
        slot = step % slots
        at = pl.ds(slot * height, span * height)
        weighted = dot_t(window_table[...], dens[at, :]) * weights[0:1, slot * height:(slot + span) * height]
        update = dot(split(weighted), dens[at, :])
        update = update[0:2 * rows] + update[2 * rows:4 * rows]
        update = update if step == 0 else totals[...] + update
        if step + span < steps:
            totals[...] = update
            return
        sums = split(update)
        by_cos = dot(sums, cos_rows[...])
        by_sin = dot(sums, sin_rows[...])
        by_cos = by_cos[0:2 * rows] + by_cos[2 * rows:4 * rows]
        by_sin = by_sin[0:2 * rows] + by_sin[2 * rows:4 * rows]
        out[0:rows, :] = by_cos[0:rows] + by_sin[rows:2 * rows]
        out[rows:2 * rows, :] = by_sin[0:rows] - by_cos[rows:2 * rows]

    @pl.when(mine > 0)
    def _():
        fill(0)

    @pl.when(is_scout & (mine > 0))
    def _():
        wait_origin()
        send_origin(hub, ic, 0, 2)

    outer = mine == steps - 1

    @pl.when(is_hub & outer)
    def _():
        fill(2)

    @pl.when(is_hub & (ic > 0))
    def _():
        wait_for(window, recv_w)
        make_window_table()

    @pl.when(is_hub & (ic == 0))
    def _():
        wait_origin()

    @pl.when(ic == 1)
    def _():
        wait_origin()

    @pl.when(is_scout & (ic == 1))
    def _():
        send_origin(hub, ic, 0, 1)


    @pl.when(mine == 0)
    def _():
        fill(0)

    def sent(conds, windows):
        def one(j):
            wait_for(gath_c.at[0], send.at[0])
            wait_for(gath_ce.at[0], send.at[0])

        each(0, conds, one)
        each(0, windows, lambda j: wait_for(window, send.at[0]))

    def wait_sent():
        wait_for(gath_v.at[pl.ds(0, nv - 1)], send.at[0])
        wait_for(gath_ve.at[pl.ds(0, nv - 1)], send.at[0])

        @pl.when(is_hub)
        def _():
            sent(jnp.maximum(ic - 1, 0), 0)

        direct = 2 - jnp.minimum(chip, 1)

        @pl.when(is_scout & (ic == 1))
        def _():
            sent(direct + 1, 1)

        @pl.when(is_scout & (ic > 1))
        def _():
            sent(direct + 2 + 2 * (nc - 1 - ic) + 1 - lax.rem(ic, 2), 1)

    def stages(ends, ahead=False, done=()):
        ends = [end for end in ends if end < steps] + list(range(slots, steps + 1, slots))
        step = filled = 0
        for end in sorted(set(ends + [steps])):
            if end == steps:
                wait_sent()
            order = list(range(max(filled, 1), min(slots, steps) if ahead and end < slots else end))
            if 1 in order and 2 in order and not ahead:
                order[0:2] = [2, 1]
            for n in order:
                if n not in done:
                    fill(n)
            filled = max([filled] + [n + 1 for n in order])
            use(step, end - step)
            step = end

    @pl.when((is_hub & (mine > 0) & (mine < steps - 1)) | (is_scout & outer))
    def _():
        stages([3])

    @pl.when(is_hub & outer)
    def _():
        stages([3], done={2})

    @pl.when(is_scout & (mine > 0) & (mine < steps - 1))
    def _():
        stages([2], ahead=True)

    @pl.when(mine == 0)
    def _():
        stages([2])


    @pl.when(is_scout & (ic == 0))
    def _():
        sent(1 + 2 * (nc - 2) + jnp.minimum(chip, 1), nc - 1)

    @pl.when(is_scout & (ic + chip > 0))
    def _():
        def one(j):
            wait_for(gath_c.at[pl.ds(0, 2)], send.at[1])
            wait_for(gath_ce.at[pl.ds(0, 2)], send.at[1])

        each(mine + 1, steps, one)


def per_device(val_orbitals, cond_orbitals, val_energy, cond_energy, wave_index):
    nv, nc = lax.axis_size("val"), lax.axis_size("cond")
    vb, points = val_orbitals.shape
    cb = cond_orbitals.shape[0]
    count = wave_index.shape[0]
    rows = NW // nv
    steps = nc // 2
    slots = min(4, steps)
    height = nv * vb * 2 * cb
    bf16, f32 = jnp.bfloat16, jnp.float32
    dma = pltpu.SemaphoreType.DMA
    regular = pltpu.SemaphoreType.REGULAR
    out = pl.pallas_call(
        functools.partial(kernel, nv, nc, slots),
        out_shape=jax.ShapeDtypeStruct((2 * rows, count), f32),
        in_specs=[pl.BlockSpec(memory_space=pltpu.HBM)] * 5,
        out_specs=pl.BlockSpec(memory_space=pltpu.VMEM),
        scratch_shapes=[
            pltpu.VMEM((nv, vb, points), bf16),
            pltpu.VMEM((nc, cb, points), bf16),
            pltpu.VMEM((nv, 1, vb), bf16),
            pltpu.VMEM((nc, 1, cb), bf16),
            pltpu.VMEM((count // LANES, LANES), jnp.int32),
            pltpu.VMEM((1, LANES), jnp.int32),
            pltpu.VMEM((points, count), bf16),
            pltpu.VMEM((points, count), bf16),
            pltpu.VMEM((2 * rows, points), bf16),
            pltpu.VMEM((slots * height, points), bf16),
            pltpu.VMEM((8, slots * height), f32),
            pltpu.VMEM((2 * rows, points), f32),
            dma, dma, dma((steps,)), dma((steps,)), dma, dma((2,)), regular((nc,)), regular, dma,
        ],
        compiler_params=pltpu.CompilerParams(
            collective_id=0, has_side_effects=True, vmem_limit_bytes=VMEM_LIMIT
        ),
    )(*[
        pltpu.with_memory_space_constraint(value, pltpu.HBM)
        for value in (
            val_orbitals, cond_orbitals, val_energy.reshape(1, vb), cond_energy.reshape(1, cb),
            wave_index.reshape(count // LANES, LANES),
        )
    ])
    factor = -4.0 / math.sqrt(nv * vb * nc * cb)
    return factor * out[0:rows], factor * out[rows:2 * rows]


def solution(mesh):
    return jax.shard_map(
        per_device,
        mesh=mesh,
        in_specs=(P("val", None), P("cond", None), P("val"), P("cond"), P("cond")),
        out_specs=(P("val", "cond"), P("val", "cond")),
        check_vma=False,
    )
```

```python
import functools
import math

import jax
import jax.numpy as jnp
from jax import lax
from jax.experimental import pallas as pl
from jax.experimental.pallas import tpu as pltpu
from jax.sharding import PartitionSpec as P

NG = 96
NW = 128
SLAB_Y = 4
LANES = 128
VMEM_LIMIT = 24 * 1024 * 1024
MESH = pl.DeviceIdType.MESH


def modulo(value, period):
    return value - period * jnp.floor((value + 0.5) * (1.0 / period))


def cos_turns(turns):
    scale = math.pi / NG
    shifted = turns - NG / 2
    square = shifted * shifted
    series = 0.0
    for order in (11, 9, 7, 5, 3, 1):
        series = series * square + (-1.0) ** (order // 2) * scale ** order / math.factorial(order)
    sine = series * shifted
    return 2.0 * sine * sine - 1.0


def wave_parts(flat):
    wave_x = jnp.floor((flat + 0.5) * (1.0 / (NG * NG)))
    rest = flat - wave_x * (NG * NG)
    wave_y = jnp.floor((rest + 0.5) * (1.0 / NG))
    return wave_x, wave_y, rest - wave_y * NG


def point_parts(point):
    plane = jnp.floor((point + 0.5) * (1.0 / NG))
    along_z = jnp.floor((plane + 0.5) * (1.0 / SLAB_Y))
    return point - plane * NG, plane - along_z * SLAB_Y, along_z


def iota(shape, axis):
    return lax.broadcasted_iota(jnp.int32, shape, axis).astype(jnp.float32)


def factors(index, points):
    wave_x, wave_y, wave_z = wave_parts(index.astype(jnp.float32))
    planes = points // NG
    along_x = iota((NG, LANES), 0)
    plane = iota((planes, LANES), 0)
    along_z = jnp.floor((plane + 0.5) * (1.0 / SLAB_Y))
    along_y = plane - along_z * SLAB_Y
    turns_x = modulo(along_x * wave_x, NG)
    turns_yz = modulo(along_y * wave_y + along_z * wave_z, NG)
    quarter = 3 * NG // 4
    return (
        cos_turns(turns_x),
        cos_turns(modulo(turns_x + quarter, NG)),
        cos_turns(turns_yz),
        cos_turns(modulo(turns_yz + quarter, NG)),
    )


def split(value):
    high = value.astype(jnp.bfloat16)
    low = (value - high.astype(jnp.float32)).astype(jnp.bfloat16)
    return jnp.concatenate([high, low], axis=0)


def dot(left, right):
    return jnp.dot(left, right, preferred_element_type=jnp.float32)


def dot_t(left, right):
    return lax.dot_general(left, right, (((1,), (1,)), ((), ())), preferred_element_type=jnp.float32)


def flip(position, size):
    if size % 2:
        return position
    return position + 1 - 2 * lax.rem(position, 2)


def nearest(position, step, size, down=False):
    both = jnp.minimum(position, size - 1 - position)
    half = (step + 1) // 2
    near = position + half if step % 2 != down else position - half
    side = jnp.where(position < size - 1 - position, 1, -1)
    return jnp.where(step <= 2 * both, near, position + side * (step - both))


def kernel(
    nv, nc, slots,
    val, cond, val_energy, cond_energy, wave, out,
    gath_v, gath_c, gath_ve, gath_ce, own_wave, window, cos_rows, sin_rows, window_table, dens, weights, totals,
    recv_v, recv_ve, recv_c, recv_ce, recv_w, send, ready, ready_v, local,
):
    iv = lax.axis_index("val")
    ic = lax.axis_index("cond")
    vb, points = val.shape
    cb = cond.shape[0]
    rows = NW // nv
    planes = points // NG
    steps = nc // 2
    mine = ic // 2
    core = lax.rem(iv, 2)
    hub = iv - core
    scout = hub + 1
    chip = iv // 2
    chips = nv // 2
    is_hub = core == 0
    is_scout = core == 1
    pairs = is_scout & (ic > 1) & (lax.rem(ic, 2) == 0)

    barrier = pltpu.get_barrier_semaphore()

    def each(first, last, body):
        def step(j, carry):
            body(j)
            return carry

        lax.fori_loop(first, last, step, 0)

    def signal(semaphore, v, c):
        pl.semaphore_signal(semaphore, inc=1, device_id={"val": v, "cond": c}, device_id_type=MESH)

    @pl.when((ic == 0) & (is_scout | (chip == 0)))
    def _():
        each(1, nc, lambda j: signal(barrier, scout, nc - j))

    @pl.when(is_scout & (ic > 0))
    def _():
        each(ic + 1, nc, lambda j: signal(barrier, hub, j))

    @pl.when(is_scout)
    def _():
        signal(barrier, hub, ic)

    each(chip + 1, chips, lambda k: signal(barrier, 2 * k, ic))

    @pl.when(ic == 0)
    def _():
        each(chip + 1, chips, lambda k: signal(barrier, 2 * k + 1, ic))


    wave_copy = pltpu.make_async_copy(wave, own_wave, local)
    own_copies = [
        pltpu.make_async_copy(cond, gath_c.at[ic], recv_c.at[mine]),
        pltpu.make_async_copy(val, gath_v.at[iv], recv_v),
        pltpu.make_async_copy(cond_energy, gath_ce.at[ic], recv_ce.at[mine]),
        pltpu.make_async_copy(val_energy, gath_ve.at[iv], recv_ve),
    ]
    wave_copy.start()
    for copy in own_copies:
        copy.start()

    def remote(v, c, src, dst, semaphore, late=0):
        pltpu.make_async_remote_copy(
            src_ref=src, dst_ref=dst, send_sem=send.at[late], recv_sem=semaphore,
            device_id={"val": v, "cond": c}, device_id_type=MESH,
        ).start()

    def send_cond(v, c):
        remote(v, c, cond, gath_c.at[ic], recv_c.at[mine])
        remote(v, c, cond_energy, gath_ce.at[ic], recv_ce.at[mine])

    def send_val(peer):
        remote(peer, ic, val, gath_v.at[iv], recv_v)
        remote(peer, ic, val_energy, gath_ve.at[iv], recv_ve)

    def send_window(v, c, source):
        remote(v, c, source, window, recv_w)

    def send_origin(v, c, first, count):
        part, energies = gath_c.at[pl.ds(first, count)], gath_ce.at[pl.ds(first, count)]
        remote(v, c, part, part, recv_c.at[0])
        remote(v, c, energies, energies, recv_ce.at[0])

    def wait_for(part, semaphore):
        pltpu.make_async_copy(part, part, semaphore).wait()

    @pl.when(is_scout & (ic > 0))
    def _():
        pl.semaphore_wait(barrier, 2 - jnp.minimum(chip, 1))
        signal(ready.at[ic], scout, 0)

        @pl.when(chip == 0)
        def _():
            send_cond(hub, 0)

        send_cond(scout, 0)

    @pl.when(is_scout & (ic == 0) & (chip > 0))
    def _():
        pl.semaphore_wait(barrier, 2 * chip)
        each(0, hub, send_val)

    @pl.when(is_hub)
    def _():
        pl.semaphore_wait(barrier, 1 + 2 * chip + jnp.maximum(ic - 1, 0))
        signal(ready.at[ic], scout, ic)
        each(2, ic, lambda j: signal(ready.at[ic], scout, j))

        each(0, hub, lambda v: signal(ready_v, v, ic))
        each(1, ic, lambda j: send_cond(scout, j))
        send_val(scout)
        each(0, hub, send_val)

    wave_copy.wait()
    for block in range(own_wave.shape[0]):
        cos_x, sin_x, cos_p, sin_p = factors(own_wave[pl.ds(block, 1), :], points)
        lanes = pl.ds(block * LANES, LANES)
        for plane in range(planes):
            at = pl.ds(plane * NG, NG)
            c, s = cos_p[plane:plane + 1, :], sin_p[plane:plane + 1, :]
            cos_rows[at, lanes] = (cos_x * c - sin_x * s).astype(jnp.bfloat16)
            sin_rows[at, lanes] = (sin_x * c + cos_x * s).astype(jnp.bfloat16)

    own_window = own_wave.at[pl.ds(0, 1)]

    def make_window_table():
        spread_wave = jnp.broadcast_to(window[...], (8, LANES))
        first = pltpu.roll(spread_wave, lax.rem(NW - iv * rows, NW), 1)
        index = jnp.broadcast_to(first[0:1, :].astype(jnp.float32), (LANES, LANES))
        wave_x, wave_y, wave_z = wave_parts(jnp.transpose(index)[0:rows])
        quarter = NG / 4
        for block in range(points // LANES):
            lanes = pl.ds(block * LANES, LANES)
            along_x, along_y, along_z = point_parts(iota((1, LANES), 1) + block * LANES)
            turns = modulo(wave_x * along_x + wave_y * along_y + wave_z * along_z, NG)
            window_table[0:rows, lanes] = cos_turns(turns).astype(jnp.bfloat16)
            turns = jnp.where(turns < quarter, turns + 3 * quarter, turns - quarter)
            window_table[rows:2 * rows, lanes] = cos_turns(turns).astype(jnp.bfloat16)

    @pl.when(ic == 0)
    def _():
        copy = pltpu.make_async_copy(own_window, window, local)
        copy.start()
        copy.wait()
        make_window_table()

    def serve(j):
        pl.semaphore_wait(ready.at[j], 1)
        send_cond(hub, j)
        send_cond(scout, j)

    @pl.when(is_scout)
    def _():
        pl.semaphore_wait(ready.at[ic], 1)
        send_val(hub)

        @pl.when(ic > 0)
        def _():
            each(0, hub, send_val)

        @pl.when(pairs)
        def _():
            serve(ic + 1)

    @pl.when(chip < chips - 1)
    def _():
        pl.semaphore_wait(ready_v, chips - 1 - chip)
        each(scout + 1, nv, send_val)

    def wait_group(g):
        wait_for(gath_c.at[pl.ds(2 * g, 2)], recv_c.at[g])
        wait_for(gath_ce.at[pl.ds(2 * g, 2)], recv_ce.at[g])

    def wait_origin():
        wait_group(0)

    @pl.when(is_scout & (ic == 0))
    def _():
        pl.semaphore_wait(ready.at[1], 1)
        send_window(scout, 1, own_window)
        send_cond(scout, 1)
        wait_origin()

        @pl.when(chip > 0)
        def _():
            send_origin(hub, 0, 1, 1)

        def serve_window(j):
            pl.semaphore_wait(ready.at[j], 1)
            send_window(scout, j, own_window)

        def send_pair(k):
            send_origin(scout, 2 * k, 0, 2)
            send_origin(scout, 2 * k + 1, 0, 2)

        def serve_pair(k):
            serve_window(2 * k)

            @pl.when(k > 1)
            def _():
                send_pair(k - 1)

            serve_window(2 * k + 1)

        each(1, steps, serve_pair)
        send_pair(steps - 1)

    @pl.when(is_scout & (ic > 1))
    def _():
        def serve_both(k):
            serve(2 * k + 1)
            serve(2 * k)

        each(mine + 1, steps, serve_both)

    @pl.when(pairs)
    def _():
        wait_group(mine)
        part, energies = gath_c.at[ic + 1], gath_ce.at[ic + 1]
        remote(hub, ic, part, part, recv_c.at[mine])
        remote(hub, ic, energies, energies, recv_ce.at[mine])

    @pl.when(is_scout & (ic > 0))
    def _():
        wait_for(window, recv_w)
        send_window(hub, ic, window)
        make_window_table()

    wait_for(gath_v, recv_v)
    wait_for(gath_ve, recv_ve)

    count = 2 * cb
    height = nv * vb * count
    pair = iota((1, height), 1)
    pair_v = jnp.floor((pair + 0.5) * (1.0 / count))
    pair_c = pair - pair_v * count

    def spread(row, length, index, offset):
        square = jnp.broadcast_to(row.astype(jnp.float32), (length, length))
        eye = iota((length, length), 0) == iota((length, length), 1)
        column = jnp.sum(jnp.where(eye, square, 0.0), axis=1, keepdims=True)
        chosen = iota((length, height), 0) + offset == index
        return jnp.sum(jnp.where(chosen, column, 0.0), axis=0, keepdims=True)

    own_val = sum(spread(gath_ve[b], vb, pair_v, b * vb) for b in range(nv))

    def fill(step):
        slot = step % slots
        if step == 0:
            other = mine

            @pl.when((mine > 0) & jnp.logical_not(pairs))
            def _():
                wait_group(mine)
        else:
            other = nearest(mine, step, steps)
            from_scout = 0 if step == 1 else nearest(mine - 1, step - 1, steps - 1) + 1
            from_hub = 0 if step == 2 else nearest(mine - 1, max(step - 1, 1), steps - 1, True) + 1
            other = jnp.where(mine > 0, jnp.where(is_hub, from_hub, from_scout), other)
            if step == 2:
                @pl.when(is_hub & (mine > 0))
                def _():
                    wait_origin()

            @pl.when(other > 0)
            def _():
                wait_group(other)

            @pl.when(is_scout & (other > mine) & (ic + chip > 0))
            def _():
                part, energies = gath_c.at[pl.ds(other * 2, 2)], gath_ce.at[pl.ds(other * 2, 2)]
                remote(hub, ic, part, part, recv_c.at[other], 1)
                remote(hub, ic, energies, energies, recv_ce.at[other], 1)

        at = [other * 2, other * 2 + 1]
        orbitals = jnp.concatenate([gath_c[j] for j in at], axis=0)
        own_cond = sum(spread(gath_ce[j], cb, pair_c, n * cb) for n, j in enumerate(at))
        weights[0:1, slot * height:(slot + 1) * height] = 1.0 / (own_cond - own_val)

        def one_block(b, carry):
            block = gath_v[b]
            for v in range(vb):
                first = pl.multiple_of(slot * height + (b * vb + v) * count, count)
                dens[pl.ds(first, count), :] = orbitals * block[v:v + 1, :]
            return carry

        lax.fori_loop(0, nv, one_block, 0, unroll=nv <= 4)

    def use(step, span):
        slot = step % slots
        at = pl.ds(slot * height, span * height)
        weighted = dot_t(window_table[...], dens[at, :]) * weights[0:1, slot * height:(slot + span) * height]
        update = dot(split(weighted), dens[at, :])
        update = update[0:2 * rows] + update[2 * rows:4 * rows]
        update = update if step == 0 else totals[...] + update
        if step + span < steps:
            totals[...] = update
            return
        sums = split(update)
        by_cos = dot(sums, cos_rows[...])
        by_sin = dot(sums, sin_rows[...])
        by_cos = by_cos[0:2 * rows] + by_cos[2 * rows:4 * rows]
        by_sin = by_sin[0:2 * rows] + by_sin[2 * rows:4 * rows]
        out[0:rows, :] = by_cos[0:rows] + by_sin[rows:2 * rows]
        out[rows:2 * rows, :] = by_sin[0:rows] - by_cos[rows:2 * rows]

    @pl.when(mine > 0)
    def _():
        fill(0)

    @pl.when(is_scout & (mine > 0))
    def _():
        wait_origin()
        send_origin(hub, ic, 0, 2)

    outer = mine == steps - 1

    @pl.when(is_hub & outer)
    def _():
        fill(1)

    @pl.when(is_hub & (ic > 0))
    def _():
        wait_for(window, recv_w)
        make_window_table()

    @pl.when(is_hub & (ic == 0))
    def _():
        wait_origin()

    @pl.when(ic == 1)
    def _():
        wait_origin()

    @pl.when(is_scout & (ic == 1))
    def _():
        send_origin(hub, ic, 0, 1)


    @pl.when(mine == 0)
    def _():
        fill(0)

    def sent(conds, windows):
        def one(j):
            wait_for(gath_c.at[0], send.at[0])
            wait_for(gath_ce.at[0], send.at[0])

        each(0, conds, one)
        each(0, windows, lambda j: wait_for(window, send.at[0]))

    def wait_sent():
        wait_for(gath_v.at[pl.ds(0, nv - 1)], send.at[0])
        wait_for(gath_ve.at[pl.ds(0, nv - 1)], send.at[0])

        @pl.when(is_hub)
        def _():
            sent(jnp.maximum(ic - 1, 0), 0)

        direct = 2 - jnp.minimum(chip, 1)

        @pl.when(is_scout & (ic == 1))
        def _():
            sent(direct + 1, 1)

        @pl.when(is_scout & (ic > 1))
        def _():
            sent(direct + 2 + 2 * (nc - 1 - ic) + 1 - lax.rem(ic, 2), 1)

    def stages(ends, ahead=False, done=()):
        ends = [end for end in ends if end < steps] + list(range(slots, steps + 1, slots))
        step = filled = 0
        for end in sorted(set(ends + [steps])):
            if end == steps:
                wait_sent()
            order = list(range(max(filled, 1), min(slots, steps) if ahead and end < slots else end))
            if 1 in order and 2 in order and not ahead:
                order[0:2] = [2, 1]
            for n in order:
                if n not in done:
                    fill(n)
            filled = max([filled] + [n + 1 for n in order])
            use(step, end - step)
            step = end

    @pl.when(is_scout & outer)
    def _():
        stages([3])

    @pl.when(is_hub & outer)
    def _():
        stages([2], done={1})

    @pl.when(is_scout & (mine > 0) & (mine < steps - 1))
    def _():
        stages([2], ahead=True)

    @pl.when(mine == 0)
    def _():
        stages([2, 3])

    @pl.when(is_hub & (mine > 0) & (mine < steps - 1))
    def _():
        stages([2])


    @pl.when(is_scout & (ic == 0))
    def _():
        sent(1 + 2 * (nc - 2) + jnp.minimum(chip, 1), nc - 1)

    @pl.when(is_scout & (ic + chip > 0))
    def _():
        def one(j):
            wait_for(gath_c.at[pl.ds(0, 2)], send.at[1])
            wait_for(gath_ce.at[pl.ds(0, 2)], send.at[1])

        each(mine + 1, steps, one)


def per_device(val_orbitals, cond_orbitals, val_energy, cond_energy, wave_index):
    nv, nc = lax.axis_size("val"), lax.axis_size("cond")
    vb, points = val_orbitals.shape
    cb = cond_orbitals.shape[0]
    count = wave_index.shape[0]
    rows = NW // nv
    steps = nc // 2
    slots = min(4, steps)
    height = nv * vb * 2 * cb
    bf16, f32 = jnp.bfloat16, jnp.float32
    dma = pltpu.SemaphoreType.DMA
    regular = pltpu.SemaphoreType.REGULAR
    out = pl.pallas_call(
        functools.partial(kernel, nv, nc, slots),
        out_shape=jax.ShapeDtypeStruct((2 * rows, count), f32),
        in_specs=[pl.BlockSpec(memory_space=pltpu.HBM)] * 5,
        out_specs=pl.BlockSpec(memory_space=pltpu.VMEM),
        scratch_shapes=[
            pltpu.VMEM((nv, vb, points), bf16),
            pltpu.VMEM((nc, cb, points), bf16),
            pltpu.VMEM((nv, 1, vb), bf16),
            pltpu.VMEM((nc, 1, cb), bf16),
            pltpu.VMEM((count // LANES, LANES), jnp.int32),
            pltpu.VMEM((1, LANES), jnp.int32),
            pltpu.VMEM((points, count), bf16),
            pltpu.VMEM((points, count), bf16),
            pltpu.VMEM((2 * rows, points), bf16),
            pltpu.VMEM((slots * height, points), bf16),
            pltpu.VMEM((8, slots * height), f32),
            pltpu.VMEM((2 * rows, points), f32),
            dma, dma, dma((steps,)), dma((steps,)), dma, dma((2,)), regular((nc,)), regular, dma,
        ],
        compiler_params=pltpu.CompilerParams(
            collective_id=0, has_side_effects=True, vmem_limit_bytes=VMEM_LIMIT
        ),
    )(*[
        pltpu.with_memory_space_constraint(value, pltpu.HBM)
        for value in (
            val_orbitals, cond_orbitals, val_energy.reshape(1, vb), cond_energy.reshape(1, cb),
            wave_index.reshape(count // LANES, LANES),
        )
    ])
    factor = -4.0 / math.sqrt(nv * vb * nc * cb)
    return factor * out[0:rows], factor * out[rows:2 * rows]


def solution(mesh):
    return jax.shard_map(
        per_device,
        mesh=mesh,
        in_specs=(P("val", None), P("cond", None), P("val"), P("cond"), P("cond")),
        out_specs=(P("val", "cond"), P("val", "cond")),
        check_vma=False,
    )
```

```python
import functools
import math

import jax
import jax.numpy as jnp
from jax import lax
from jax.experimental import pallas as pl
from jax.experimental.pallas import tpu as pltpu
from jax.sharding import PartitionSpec as P

NG = 96
NW = 128
SLAB_Y = 4
LANES = 128
VMEM_LIMIT = 24 * 1024 * 1024
MESH = pl.DeviceIdType.MESH


def modulo(value, period):
    return value - period * jnp.floor((value + 0.5) * (1.0 / period))


def cos_turns(turns):
    scale = math.pi / NG
    shifted = turns - NG / 2
    square = shifted * shifted
    series = 0.0
    for order in (11, 9, 7, 5, 3, 1):
        series = series * square + (-1.0) ** (order // 2) * scale ** order / math.factorial(order)
    sine = series * shifted
    return 2.0 * sine * sine - 1.0


def wave_parts(flat):
    wave_x = jnp.floor((flat + 0.5) * (1.0 / (NG * NG)))
    rest = flat - wave_x * (NG * NG)
    wave_y = jnp.floor((rest + 0.5) * (1.0 / NG))
    return wave_x, wave_y, rest - wave_y * NG


def point_parts(point):
    plane = jnp.floor((point + 0.5) * (1.0 / NG))
    along_z = jnp.floor((plane + 0.5) * (1.0 / SLAB_Y))
    return point - plane * NG, plane - along_z * SLAB_Y, along_z


def iota(shape, axis):
    return lax.broadcasted_iota(jnp.int32, shape, axis).astype(jnp.float32)


def factors(index, points):
    wave_x, wave_y, wave_z = wave_parts(index.astype(jnp.float32))
    planes = points // NG
    along_x = iota((NG, LANES), 0)
    plane = iota((planes, LANES), 0)
    along_z = jnp.floor((plane + 0.5) * (1.0 / SLAB_Y))
    along_y = plane - along_z * SLAB_Y
    turns_x = modulo(along_x * wave_x, NG)
    turns_yz = modulo(along_y * wave_y + along_z * wave_z, NG)
    quarter = 3 * NG // 4
    return (
        cos_turns(turns_x),
        cos_turns(modulo(turns_x + quarter, NG)),
        cos_turns(turns_yz),
        cos_turns(modulo(turns_yz + quarter, NG)),
    )


def split(value):
    high = value.astype(jnp.bfloat16)
    low = (value - high.astype(jnp.float32)).astype(jnp.bfloat16)
    return jnp.concatenate([high, low], axis=0)


def dot(left, right):
    return jnp.dot(left, right, preferred_element_type=jnp.float32)


def dot_t(left, right):
    return lax.dot_general(left, right, (((1,), (1,)), ((), ())), preferred_element_type=jnp.float32)


def flip(position, size):
    if size % 2:
        return position
    return position + 1 - 2 * lax.rem(position, 2)


def nearest(position, step, size, down=False):
    both = jnp.minimum(position, size - 1 - position)
    half = (step + 1) // 2
    near = position + half if step % 2 != down else position - half
    side = jnp.where(position < size - 1 - position, 1, -1)
    return jnp.where(step <= 2 * both, near, position + side * (step - both))


def kernel(
    nv, nc, slots,
    val, cond, val_energy, cond_energy, wave, out,
    gath_v, gath_c, gath_ve, gath_ce, own_wave, window, cos_rows, sin_rows, window_table, dens, weights, totals,
    recv_v, recv_ve, recv_c, recv_ce, recv_w, send, ready, local,
):
    iv = lax.axis_index("val")
    ic = lax.axis_index("cond")
    vb, points = val.shape
    cb = cond.shape[0]
    rows = NW // nv
    planes = points // NG
    steps = nc // 2
    mine = ic // 2
    core = lax.rem(iv, 2)
    hub = iv - core
    scout = hub + 1
    chip = iv // 2
    chips = nv // 2
    is_hub = core == 0
    is_scout = core == 1
    pairs = is_scout & (ic > 1) & (lax.rem(ic, 2) == 0)

    barrier = pltpu.get_barrier_semaphore()

    def each(first, last, body):
        def step(j, carry):
            body(j)
            return carry

        lax.fori_loop(first, last, step, 0)

    def signal(semaphore, v, c):
        pl.semaphore_signal(semaphore, inc=1, device_id={"val": v, "cond": c}, device_id_type=MESH)

    @pl.when((ic == 0) & (is_scout | (chip == 0)))
    def _():
        each(1, nc, lambda j: signal(barrier, scout, nc - j))

    def remote(v, c, src, dst, semaphore, sent_on=send):
        pltpu.make_async_remote_copy(
            src_ref=src, dst_ref=dst, send_sem=sent_on, recv_sem=semaphore,
            device_id={"val": v, "cond": c}, device_id_type=MESH,
        ).start()

    def send_cond(v, c):
        remote(v, c, cond, gath_c.at[ic], recv_c.at[mine])
        remote(v, c, cond_energy, gath_ce.at[ic], recv_ce.at[mine])

    @pl.when(is_scout & (ic > 0))
    def _():
        pl.semaphore_wait(barrier, 2 - jnp.minimum(chip, 1))

        @pl.when(chip == 0)
        def _():
            send_cond(hub, 0)

        signal(ready.at[ic], scout, 0)
        send_cond(scout, 0)
        each(ic + 1, nc, lambda j: signal(barrier, hub, j))

    @pl.when(is_scout)
    def _():
        signal(barrier, hub, ic)

    each(chip + 1, chips, lambda k: signal(barrier, 2 * k, ic))

    @pl.when(ic == 0)
    def _():
        each(chip + 1, chips, lambda k: signal(barrier, 2 * k + 1, ic))


    wave_copy = pltpu.make_async_copy(wave, own_wave, local)
    own_copies = [
        pltpu.make_async_copy(cond, gath_c.at[ic], recv_c.at[mine]),
        pltpu.make_async_copy(val, gath_v.at[iv], recv_v),
        pltpu.make_async_copy(cond_energy, gath_ce.at[ic], recv_ce.at[mine]),
        pltpu.make_async_copy(val_energy, gath_ve.at[iv], recv_ve),
    ]
    wave_copy.start()
    for copy in own_copies:
        copy.start()

    def send_val(peer):
        remote(peer, ic, val, gath_v.at[iv], recv_v)
        remote(peer, ic, val_energy, gath_ve.at[iv], recv_ve)

    def send_window(v, c, source):
        remote(v, c, source, window, recv_w)

    def send_origin(v, c, first, count):
        part, energies = gath_c.at[pl.ds(first, count)], gath_ce.at[pl.ds(first, count)]
        remote(v, c, part, part, recv_c.at[0])
        remote(v, c, energies, energies, recv_ce.at[0])

    def wait_for(part, semaphore):
        pltpu.make_async_copy(part, part, semaphore).wait()

    @pl.when(is_scout & (ic == 0) & (chip > 0))
    def _():
        pl.semaphore_wait(barrier, 2 * chip)
        each(0, hub, send_val)

    @pl.when(is_hub)
    def _():
        pl.semaphore_wait(barrier, 1 + 2 * chip + jnp.maximum(ic - 1, 0))
        signal(ready.at[ic], scout, ic)
        each(2, ic, lambda j: signal(ready.at[ic], scout, j))

        each(0, hub, lambda v: signal(ready.at[ic], v, ic))
        each(1, ic, lambda j: send_cond(scout, j))
        send_val(scout)
        each(0, hub, send_val)

    wave_copy.wait()
    for block in range(own_wave.shape[0]):
        cos_x, sin_x, cos_p, sin_p = factors(own_wave[pl.ds(block, 1), :], points)
        lanes = pl.ds(block * LANES, LANES)
        for plane in range(planes):
            at = pl.ds(plane * NG, NG)
            c, s = cos_p[plane:plane + 1, :], sin_p[plane:plane + 1, :]
            cos_rows[at, lanes] = (cos_x * c - sin_x * s).astype(jnp.bfloat16)
            sin_rows[at, lanes] = (sin_x * c + cos_x * s).astype(jnp.bfloat16)

    own_window = own_wave.at[pl.ds(0, 1)]

    def make_window_table():
        spread_wave = jnp.broadcast_to(window[...], (8, LANES))
        first = pltpu.roll(spread_wave, lax.rem(NW - iv * rows, NW), 1)
        index = jnp.broadcast_to(first[0:1, :].astype(jnp.float32), (LANES, LANES))
        wave_x, wave_y, wave_z = wave_parts(jnp.transpose(index)[0:rows])
        quarter = NG / 4
        for block in range(points // LANES):
            lanes = pl.ds(block * LANES, LANES)
            along_x, along_y, along_z = point_parts(iota((1, LANES), 1) + block * LANES)
            turns = modulo(wave_x * along_x + wave_y * along_y + wave_z * along_z, NG)
            window_table[0:rows, lanes] = cos_turns(turns).astype(jnp.bfloat16)
            turns = jnp.where(turns < quarter, turns + 3 * quarter, turns - quarter)
            window_table[rows:2 * rows, lanes] = cos_turns(turns).astype(jnp.bfloat16)

    @pl.when(ic == 0)
    def _():
        copy = pltpu.make_async_copy(own_window, window, local)
        copy.start()
        copy.wait()
        make_window_table()

    def serve(j):
        pl.semaphore_wait(ready.at[j], 1)
        send_cond(hub, j)
        send_cond(scout, j)

    @pl.when(pairs)
    def _():
        serve(ic + 1)

    expected = chips - 1 - chip + core

    @pl.when(expected > 0)
    def _():
        pl.semaphore_wait(ready.at[ic], expected)

    @pl.when(is_scout)
    def _():
        send_val(hub)

        @pl.when(ic > 0)
        def _():
            each(0, hub, send_val)

    each(scout + 1, nv, send_val)

    def wait_group(g):
        wait_for(gath_c.at[pl.ds(2 * g, 2)], recv_c.at[g])
        wait_for(gath_ce.at[pl.ds(2 * g, 2)], recv_ce.at[g])

    def wait_origin():
        wait_group(0)

    @pl.when(is_scout & (ic == 0))
    def _():
        pl.semaphore_wait(ready.at[1], 1)
        send_window(scout, 1, own_window)
        send_cond(scout, 1)
        wait_origin()

        @pl.when(chip > 0)
        def _():
            send_origin(hub, 0, 1, 1)

        def serve_window(j):
            pl.semaphore_wait(ready.at[j], 1)
            send_window(scout, j, own_window)

        def send_pair(k):
            send_origin(scout, 2 * k, 0, 2)
            send_origin(scout, 2 * k + 1, 0, 2)

        def serve_pair(k):
            serve_window(2 * k)

            @pl.when(k > 1)
            def _():
                send_pair(k - 1)

            serve_window(2 * k + 1)

        each(1, steps, serve_pair)
        send_pair(steps - 1)

    @pl.when(is_scout & (ic > 1))
    def _():
        def serve_both(k):
            serve(2 * k + 1)
            serve(2 * k)

        each(mine + 1, steps, serve_both)

    @pl.when(pairs)
    def _():
        wait_group(mine)
        part, energies = gath_c.at[ic + 1], gath_ce.at[ic + 1]
        remote(hub, ic, part, part, recv_c.at[mine])
        remote(hub, ic, energies, energies, recv_ce.at[mine])

    @pl.when(is_scout & (ic > 0))
    def _():
        wait_for(window, recv_w)
        send_window(hub, ic, window)
        make_window_table()

    wait_for(gath_v, recv_v)
    wait_for(gath_ve, recv_ve)

    count = 2 * cb
    height = nv * vb * count
    pair = iota((1, height), 1)
    pair_v = jnp.floor((pair + 0.5) * (1.0 / count))
    pair_c = pair - pair_v * count

    def spread(row, length, index, offset):
        square = jnp.broadcast_to(row.astype(jnp.float32), (length, length))
        eye = iota((length, length), 0) == iota((length, length), 1)
        column = jnp.sum(jnp.where(eye, square, 0.0), axis=1, keepdims=True)
        chosen = iota((length, height), 0) + offset == index
        return jnp.sum(jnp.where(chosen, column, 0.0), axis=0, keepdims=True)

    own_val = sum(spread(gath_ve[b], vb, pair_v, b * vb) for b in range(nv))

    def fill(step):
        slot = step % slots
        if step == 0:
            other = mine

            @pl.when((mine > 0) & jnp.logical_not(pairs))
            def _():
                wait_group(mine)
        else:
            other = nearest(mine, step, steps)
            from_scout = 0 if step == 1 else nearest(mine - 1, step - 1, steps - 1) + 1
            from_hub = 0 if step == 2 else nearest(mine - 1, max(step - 1, 1), steps - 1, True) + 1
            other = jnp.where(mine > 0, jnp.where(is_hub, from_hub, from_scout), other)
            if step == 2:
                @pl.when(is_hub & (mine > 0))
                def _():
                    wait_origin()

            @pl.when(other > 0)
            def _():
                wait_group(other)

            @pl.when(is_scout & (other > mine) & (ic + chip > 0))
            def _():
                part, energies = gath_c.at[pl.ds(other * 2, 2)], gath_ce.at[pl.ds(other * 2, 2)]
                remote(hub, ic, part, part, recv_c.at[other], local)
                remote(hub, ic, energies, energies, recv_ce.at[other], local)

        at = [other * 2, other * 2 + 1]
        orbitals = jnp.concatenate([gath_c[j] for j in at], axis=0)
        own_cond = sum(spread(gath_ce[j], cb, pair_c, n * cb) for n, j in enumerate(at))
        weights[0:1, slot * height:(slot + 1) * height] = 1.0 / (own_cond - own_val)

        def one_block(b, carry):
            block = gath_v[b]
            for v in range(vb):
                first = pl.multiple_of(slot * height + (b * vb + v) * count, count)
                dens[pl.ds(first, count), :] = orbitals * block[v:v + 1, :]
            return carry

        lax.fori_loop(0, nv, one_block, 0, unroll=nv <= 4)

    def use(step, span):
        slot = step % slots
        at = pl.ds(slot * height, span * height)
        weighted = dot_t(window_table[...], dens[at, :]) * weights[0:1, slot * height:(slot + span) * height]
        update = dot(split(weighted), dens[at, :])
        update = update[0:2 * rows] + update[2 * rows:4 * rows]
        update = update if step == 0 else totals[...] + update
        if step + span < steps:
            totals[...] = update
            return
        sums = split(update)
        by_cos = dot(sums, cos_rows[...])
        by_sin = dot(sums, sin_rows[...])
        by_cos = by_cos[0:2 * rows] + by_cos[2 * rows:4 * rows]
        by_sin = by_sin[0:2 * rows] + by_sin[2 * rows:4 * rows]
        out[0:rows, :] = by_cos[0:rows] + by_sin[rows:2 * rows]
        out[rows:2 * rows, :] = by_sin[0:rows] - by_cos[rows:2 * rows]

    @pl.when(mine > 0)
    def _():
        fill(0)

    @pl.when(is_scout & (mine > 0))
    def _():
        wait_origin()
        send_origin(hub, ic, 0, 2)

    outer = mine == steps - 1

    @pl.when(is_hub & outer)
    def _():
        fill(1)

    @pl.when(is_hub & (ic > 0))
    def _():
        wait_for(window, recv_w)
        make_window_table()

    @pl.when(is_hub & (ic == 0))
    def _():
        wait_origin()

    @pl.when(ic == 1)
    def _():
        wait_origin()

    @pl.when(is_scout & (ic == 1))
    def _():
        send_origin(hub, ic, 0, 1)


    @pl.when(mine == 0)
    def _():
        fill(0)

    def sent(conds, windows):
        def one(j):
            wait_for(gath_c.at[0], send)
            wait_for(gath_ce.at[0], send)

        each(0, conds, one)
        each(0, windows, lambda j: wait_for(window, send))

    def wait_sent():
        wait_for(gath_v.at[pl.ds(0, nv - 1)], send)
        wait_for(gath_ve.at[pl.ds(0, nv - 1)], send)

        @pl.when(is_hub)
        def _():
            sent(jnp.maximum(ic - 1, 0), 0)

        direct = 2 - jnp.minimum(chip, 1)

        @pl.when(is_scout & (ic == 1))
        def _():
            sent(direct + 1, 1)

        @pl.when(is_scout & (ic > 1))
        def _():
            sent(direct + 2 + 2 * (nc - 1 - ic) + 1 - lax.rem(ic, 2), 1)

    def stages(ends, ahead=False, done=()):
        ends = [end for end in ends if end < steps] + list(range(slots, steps + 1, slots))
        step = filled = 0
        for end in sorted(set(ends + [steps])):
            if end == steps:
                wait_sent()
            order = list(range(max(filled, 1), min(slots, steps) if ahead and end < slots else end))
            if 1 in order and 2 in order and not ahead:
                order[0:2] = [2, 1]
            for n in order:
                if n not in done:
                    fill(n)
            filled = max([filled] + [n + 1 for n in order])
            use(step, end - step)
            step = end

    @pl.when(is_scout & outer)
    def _():
        stages([3])

    @pl.when(is_hub & outer)
    def _():
        stages([2], done={1})

    @pl.when(is_scout & (mine > 0) & (mine < steps - 1))
    def _():
        stages([2], ahead=True)

    @pl.when(mine == 0)
    def _():
        stages([2, 3])

    @pl.when(is_hub & (mine > 0) & (mine < steps - 1))
    def _():
        stages([2])


    @pl.when(is_scout & (ic == 0))
    def _():
        sent(1 + 2 * (nc - 2) + jnp.minimum(chip, 1), nc - 1)

    @pl.when(is_scout & (ic + chip > 0))
    def _():
        def one(j):
            wait_for(gath_c.at[pl.ds(0, 2)], local)
            wait_for(gath_ce.at[pl.ds(0, 2)], local)

        each(mine + 1, steps, one)


def per_device(val_orbitals, cond_orbitals, val_energy, cond_energy, wave_index):
    nv, nc = lax.axis_size("val"), lax.axis_size("cond")
    vb, points = val_orbitals.shape
    cb = cond_orbitals.shape[0]
    count = wave_index.shape[0]
    rows = NW // nv
    steps = nc // 2
    slots = min(4, steps)
    height = nv * vb * 2 * cb
    bf16, f32 = jnp.bfloat16, jnp.float32
    dma = pltpu.SemaphoreType.DMA
    regular = pltpu.SemaphoreType.REGULAR
    out = pl.pallas_call(
        functools.partial(kernel, nv, nc, slots),
        out_shape=jax.ShapeDtypeStruct((2 * rows, count), f32),
        in_specs=[pl.BlockSpec(memory_space=pltpu.HBM)] * 5,
        out_specs=pl.BlockSpec(memory_space=pltpu.VMEM),
        scratch_shapes=[
            pltpu.VMEM((nv, vb, points), bf16),
            pltpu.VMEM((nc, cb, points), bf16),
            pltpu.VMEM((nv, 1, vb), bf16),
            pltpu.VMEM((nc, 1, cb), bf16),
            pltpu.VMEM((count // LANES, LANES), jnp.int32),
            pltpu.VMEM((1, LANES), jnp.int32),
            pltpu.VMEM((points, count), bf16),
            pltpu.VMEM((points, count), bf16),
            pltpu.VMEM((2 * rows, points), bf16),
            pltpu.VMEM((slots * height, points), bf16),
            pltpu.VMEM((8, slots * height), f32),
            pltpu.VMEM((2 * rows, points), f32),
            dma, dma, dma((steps,)), dma((steps,)), dma, dma, regular((nc,)), dma,
        ],
        compiler_params=pltpu.CompilerParams(
            collective_id=0, has_side_effects=True, vmem_limit_bytes=VMEM_LIMIT
        ),
    )(*[
        pltpu.with_memory_space_constraint(value, pltpu.HBM)
        for value in (
            val_orbitals, cond_orbitals, val_energy.reshape(1, vb), cond_energy.reshape(1, cb),
            wave_index.reshape(count // LANES, LANES),
        )
    ])
    factor = -4.0 / math.sqrt(nv * vb * nc * cb)
    return factor * out[0:rows], factor * out[rows:2 * rows]


def solution(mesh):
    return jax.shard_map(
        per_device,
        mesh=mesh,
        in_specs=(P("val", None), P("cond", None), P("val"), P("cond"), P("cond")),
        out_specs=(P("val", "cond"), P("val", "cond")),
        check_vma=False,
    )
```

```python
import functools
import math

import jax
import jax.numpy as jnp
from jax import lax
from jax.experimental import pallas as pl
from jax.experimental.pallas import tpu as pltpu
from jax.sharding import PartitionSpec as P

NG = 96
NW = 128
SLAB_Y = 4
LANES = 128
VMEM_LIMIT = 24 * 1024 * 1024
MESH = pl.DeviceIdType.MESH


def modulo(value, period):
    return value - period * jnp.floor((value + 0.5) * (1.0 / period))


def cos_turns(turns):
    scale = math.pi / NG
    shifted = turns - NG / 2
    square = shifted * shifted
    series = 0.0
    for order in (11, 9, 7, 5, 3, 1):
        series = series * square + (-1.0) ** (order // 2) * scale ** order / math.factorial(order)
    sine = series * shifted
    return 2.0 * sine * sine - 1.0


def wave_parts(flat):
    wave_x = jnp.floor((flat + 0.5) * (1.0 / (NG * NG)))
    rest = flat - wave_x * (NG * NG)
    wave_y = jnp.floor((rest + 0.5) * (1.0 / NG))
    return wave_x, wave_y, rest - wave_y * NG


def point_parts(point):
    plane = jnp.floor((point + 0.5) * (1.0 / NG))
    along_z = jnp.floor((plane + 0.5) * (1.0 / SLAB_Y))
    return point - plane * NG, plane - along_z * SLAB_Y, along_z


def iota(shape, axis):
    return lax.broadcasted_iota(jnp.int32, shape, axis).astype(jnp.float32)


def factors(index, points):
    wave_x, wave_y, wave_z = wave_parts(index.astype(jnp.float32))
    planes = points // NG
    along_x = iota((NG, LANES), 0)
    plane = iota((planes, LANES), 0)
    along_z = jnp.floor((plane + 0.5) * (1.0 / SLAB_Y))
    along_y = plane - along_z * SLAB_Y
    turns_x = modulo(along_x * wave_x, NG)
    turns_yz = modulo(along_y * wave_y + along_z * wave_z, NG)
    quarter = 3 * NG // 4
    return (
        cos_turns(turns_x),
        cos_turns(modulo(turns_x + quarter, NG)),
        cos_turns(turns_yz),
        cos_turns(modulo(turns_yz + quarter, NG)),
    )


def split(value):
    high = value.astype(jnp.bfloat16)
    low = (value - high.astype(jnp.float32)).astype(jnp.bfloat16)
    return jnp.concatenate([high, low], axis=0)


def dot(left, right):
    return jnp.dot(left, right, preferred_element_type=jnp.float32)


def dot_t(left, right):
    return lax.dot_general(left, right, (((1,), (1,)), ((), ())), preferred_element_type=jnp.float32)


def flip(position, size):
    if size % 2:
        return position
    return position + 1 - 2 * lax.rem(position, 2)


def nearest(position, step, size, down=False):
    both = jnp.minimum(position, size - 1 - position)
    half = (step + 1) // 2
    near = position + half if step % 2 != down else position - half
    side = jnp.where(position < size - 1 - position, 1, -1)
    return jnp.where(step <= 2 * both, near, position + side * (step - both))


def kernel(
    nv, nc, slots,
    val, cond, val_energy, cond_energy, wave, out,
    gath_v, gath_c, gath_ve, gath_ce, own_wave, window, cos_rows, sin_rows, window_table, dens, weights, totals,
    recv_v, recv_ve, recv_c, recv_ce, recv_w, send, ready, local,
):
    iv = lax.axis_index("val")
    ic = lax.axis_index("cond")
    vb, points = val.shape
    cb = cond.shape[0]
    rows = NW // nv
    planes = points // NG
    steps = nc // 2
    mine = ic // 2
    core = lax.rem(iv, 2)
    hub = iv - core
    scout = hub + 1
    chip = iv // 2
    chips = nv // 2
    is_hub = core == 0
    is_scout = core == 1
    pairs = is_scout & (ic > 1) & (lax.rem(ic, 2) == 0)

    barrier = pltpu.get_barrier_semaphore()

    def each(first, last, body):
        def step(j, carry):
            body(j)
            return carry

        lax.fori_loop(first, last, step, 0)

    def signal(semaphore, v, c):
        pl.semaphore_signal(semaphore, inc=1, device_id={"val": v, "cond": c}, device_id_type=MESH)

    @pl.when((ic == 0) & (is_scout | (chip == 0)))
    def _():
        each(1, nc, lambda j: signal(barrier, scout, nc - j))

    def remote(v, c, src, dst, semaphore, sent_on=send):
        pltpu.make_async_remote_copy(
            src_ref=src, dst_ref=dst, send_sem=sent_on, recv_sem=semaphore,
            device_id={"val": v, "cond": c}, device_id_type=MESH,
        ).start()

    def send_cond(v, c):
        remote(v, c, cond, gath_c.at[ic], recv_c.at[mine])
        remote(v, c, cond_energy, gath_ce.at[ic], recv_ce.at[mine])

    @pl.when(is_scout & (ic > 0))
    def _():
        pl.semaphore_wait(barrier, 2 - jnp.minimum(chip, 1))

        @pl.when(chip == 0)
        def _():
            remote(hub, 0, cond_energy, gath_ce.at[ic], recv_ce.at[mine])
            remote(hub, 0, cond, gath_c.at[ic], recv_c.at[mine])

        signal(ready.at[ic], scout, 0)
        send_cond(scout, 0)
        each(ic + 1, nc, lambda j: signal(barrier, hub, j))

    @pl.when(is_scout)
    def _():
        signal(barrier, hub, ic)

    each(chip + 1, chips, lambda k: signal(barrier, 2 * k, ic))

    @pl.when(ic == 0)
    def _():
        each(chip + 1, chips, lambda k: signal(barrier, 2 * k + 1, ic))


    wave_copy = pltpu.make_async_copy(wave, own_wave, local)
    own_copies = [
        pltpu.make_async_copy(cond, gath_c.at[ic], recv_c.at[mine]),
        pltpu.make_async_copy(val, gath_v.at[iv], recv_v),
        pltpu.make_async_copy(cond_energy, gath_ce.at[ic], recv_ce.at[mine]),
        pltpu.make_async_copy(val_energy, gath_ve.at[iv], recv_ve),
    ]
    wave_copy.start()
    for copy in own_copies:
        copy.start()

    def send_val(peer):
        remote(peer, ic, val, gath_v.at[iv], recv_v)
        remote(peer, ic, val_energy, gath_ve.at[iv], recv_ve)

    def send_window(v, c, source):
        remote(v, c, source, window, recv_w)

    def send_origin(v, c, first, count):
        part, energies = gath_c.at[pl.ds(first, count)], gath_ce.at[pl.ds(first, count)]
        remote(v, c, part, part, recv_c.at[0])
        remote(v, c, energies, energies, recv_ce.at[0])

    def wait_for(part, semaphore):
        pltpu.make_async_copy(part, part, semaphore).wait()

    @pl.when(is_scout & (ic == 0) & (chip > 0))
    def _():
        pl.semaphore_wait(barrier, 2 * chip)
        each(0, hub, send_val)

    @pl.when(is_hub)
    def _():
        pl.semaphore_wait(barrier, 1 + 2 * chip + jnp.maximum(ic - 1, 0))
        signal(ready.at[ic], scout, ic)
        each(2, ic, lambda j: signal(ready.at[ic], scout, j))

        each(0, hub, lambda v: signal(ready.at[ic], v, ic))
        each(1, ic, lambda j: send_cond(scout, j))
        send_val(scout)
        each(0, hub, send_val)

    wave_copy.wait()
    for block in range(own_wave.shape[0]):
        cos_x, sin_x, cos_p, sin_p = factors(own_wave[pl.ds(block, 1), :], points)
        lanes = pl.ds(block * LANES, LANES)
        for plane in range(planes):
            at = pl.ds(plane * NG, NG)
            c, s = cos_p[plane:plane + 1, :], sin_p[plane:plane + 1, :]
            cos_rows[at, lanes] = (cos_x * c - sin_x * s).astype(jnp.bfloat16)
            sin_rows[at, lanes] = (sin_x * c + cos_x * s).astype(jnp.bfloat16)

    own_window = own_wave.at[pl.ds(0, 1)]

    def make_window_table():
        spread_wave = jnp.broadcast_to(window[...], (8, LANES))
        first = pltpu.roll(spread_wave, lax.rem(NW - iv * rows, NW), 1)
        index = jnp.broadcast_to(first[0:1, :].astype(jnp.float32), (LANES, LANES))
        wave_x, wave_y, wave_z = wave_parts(jnp.transpose(index)[0:rows])
        quarter = NG / 4
        for block in range(points // LANES):
            lanes = pl.ds(block * LANES, LANES)
            along_x, along_y, along_z = point_parts(iota((1, LANES), 1) + block * LANES)
            turns = modulo(wave_x * along_x + wave_y * along_y + wave_z * along_z, NG)
            window_table[0:rows, lanes] = cos_turns(turns).astype(jnp.bfloat16)
            turns = jnp.where(turns < quarter, turns + 3 * quarter, turns - quarter)
            window_table[rows:2 * rows, lanes] = cos_turns(turns).astype(jnp.bfloat16)

    @pl.when(ic == 0)
    def _():
        copy = pltpu.make_async_copy(own_window, window, local)
        copy.start()
        copy.wait()
        make_window_table()

    def serve(j):
        pl.semaphore_wait(ready.at[j], 1)
        send_cond(hub, j)
        send_cond(scout, j)

    @pl.when(pairs)
    def _():
        serve(ic + 1)

    expected = chips - 1 - chip + core

    @pl.when(expected > 0)
    def _():
        pl.semaphore_wait(ready.at[ic], expected)

    @pl.when(is_scout)
    def _():
        send_val(hub)

        @pl.when(ic > 0)
        def _():
            each(0, hub, send_val)

    each(scout + 1, nv, send_val)

    def wait_group(g):
        wait_for(gath_c.at[pl.ds(2 * g, 2)], recv_c.at[g])
        wait_for(gath_ce.at[pl.ds(2 * g, 2)], recv_ce.at[g])

    def wait_origin():
        wait_group(0)

    @pl.when(is_scout & (ic == 0))
    def _():
        pl.semaphore_wait(ready.at[1], 1)
        send_window(scout, 1, own_window)
        send_cond(scout, 1)
        wait_origin()

        @pl.when(chip > 0)
        def _():
            send_origin(hub, 0, 1, 1)

        def serve_window(j):
            pl.semaphore_wait(ready.at[j], 1)
            send_window(scout, j, own_window)

        def send_pair(k):
            send_origin(scout, 2 * k, 0, 2)
            send_origin(scout, 2 * k + 1, 0, 2)

        def serve_pair(k):
            serve_window(2 * k)

            @pl.when(k > 1)
            def _():
                send_pair(k - 1)

            serve_window(2 * k + 1)

        each(1, steps, serve_pair)
        send_pair(steps - 1)

    @pl.when(is_scout & (ic > 1))
    def _():
        def serve_both(k):
            serve(2 * k + 1)
            serve(2 * k)

        each(mine + 1, steps, serve_both)

    @pl.when(pairs)
    def _():
        wait_group(mine)
        part, energies = gath_c.at[ic + 1], gath_ce.at[ic + 1]
        remote(hub, ic, part, part, recv_c.at[mine])
        remote(hub, ic, energies, energies, recv_ce.at[mine])

    @pl.when(is_scout & (ic > 0))
    def _():
        wait_for(window, recv_w)
        send_window(hub, ic, window)
        make_window_table()

    wait_for(gath_v, recv_v)
    wait_for(gath_ve, recv_ve)

    count = 2 * cb
    height = nv * vb * count
    pair = iota((1, height), 1)
    pair_v = jnp.floor((pair + 0.5) * (1.0 / count))
    pair_c = pair - pair_v * count

    def spread(row, length, index, offset):
        square = jnp.broadcast_to(row.astype(jnp.float32), (length, length))
        eye = iota((length, length), 0) == iota((length, length), 1)
        column = jnp.sum(jnp.where(eye, square, 0.0), axis=1, keepdims=True)
        chosen = iota((length, height), 0) + offset == index
        return jnp.sum(jnp.where(chosen, column, 0.0), axis=0, keepdims=True)

    own_val = sum(spread(gath_ve[b], vb, pair_v, b * vb) for b in range(nv))

    def fill(step):
        slot = step % slots
        if step == 0:
            other = mine

            @pl.when((mine > 0) & jnp.logical_not(pairs))
            def _():
                wait_group(mine)
        else:
            other = nearest(mine, step, steps)
            from_scout = 0 if step == 1 else nearest(mine - 1, step - 1, steps - 1) + 1
            from_hub = 0 if step == 2 else nearest(mine - 1, max(step - 1, 1), steps - 1, True) + 1
            other = jnp.where(mine > 0, jnp.where(is_hub, from_hub, from_scout), other)

            @pl.when(is_hub & (mine > 0) & (other == 0))
            def _():
                wait_origin()

            @pl.when(other > 0)
            def _():
                wait_group(other)

            @pl.when(is_scout & (other > mine) & (ic + chip > 0))
            def _():
                part, energies = gath_c.at[pl.ds(other * 2, 2)], gath_ce.at[pl.ds(other * 2, 2)]
                remote(hub, ic, part, part, recv_c.at[other], local)
                remote(hub, ic, energies, energies, recv_ce.at[other], local)

        at = [other * 2, other * 2 + 1]
        orbitals = jnp.concatenate([gath_c[j] for j in at], axis=0)
        own_cond = sum(spread(gath_ce[j], cb, pair_c, n * cb) for n, j in enumerate(at))
        weights[0:1, slot * height:(slot + 1) * height] = 1.0 / (own_cond - own_val)

        def one_block(b, carry):
            block = gath_v[b]
            for v in range(vb):
                first = pl.multiple_of(slot * height + (b * vb + v) * count, count)
                dens[pl.ds(first, count), :] = orbitals * block[v:v + 1, :]
            return carry

        lax.fori_loop(0, nv, one_block, 0, unroll=nv <= 4)

    def use(step, span):
        slot = step % slots
        at = pl.ds(slot * height, span * height)
        weighted = dot_t(window_table[...], dens[at, :]) * weights[0:1, slot * height:(slot + span) * height]
        update = dot(split(weighted), dens[at, :])
        update = update[0:2 * rows] + update[2 * rows:4 * rows]
        update = update if step == 0 else totals[...] + update
        if step + span < steps:
            totals[...] = update
            return
        sums = split(update)
        by_cos = dot(sums, cos_rows[...])
        by_sin = dot(sums, sin_rows[...])
        by_cos = by_cos[0:2 * rows] + by_cos[2 * rows:4 * rows]
        by_sin = by_sin[0:2 * rows] + by_sin[2 * rows:4 * rows]
        out[0:rows, :] = by_cos[0:rows] + by_sin[rows:2 * rows]
        out[rows:2 * rows, :] = by_sin[0:rows] - by_cos[rows:2 * rows]

    @pl.when(mine > 0)
    def _():
        fill(0)

    @pl.when(is_scout & (mine > 0))
    def _():
        wait_origin()
        send_origin(hub, ic, 0, 2)

    outer = mine == steps - 1

    @pl.when(is_hub & outer)
    def _():
        fill(1)

    @pl.when(is_hub & (ic > 0))
    def _():
        wait_for(window, recv_w)
        make_window_table()

    @pl.when(is_hub & (ic == 0))
    def _():
        wait_origin()

    @pl.when(ic == 1)
    def _():
        wait_origin()

    @pl.when(is_scout & (ic == 1))
    def _():
        send_origin(hub, ic, 0, 1)


    @pl.when(mine == 0)
    def _():
        fill(0)

    def sent(conds, windows):
        def one(j):
            wait_for(gath_c.at[0], send)
            wait_for(gath_ce.at[0], send)

        each(0, conds, one)
        each(0, windows, lambda j: wait_for(window, send))

    def wait_sent():
        wait_for(gath_v.at[pl.ds(0, nv - 1)], send)
        wait_for(gath_ve.at[pl.ds(0, nv - 1)], send)

        @pl.when(is_hub)
        def _():
            sent(jnp.maximum(ic - 1, 0), 0)

        direct = 2 - jnp.minimum(chip, 1)

        @pl.when(is_scout & (ic == 1))
        def _():
            sent(direct + 1, 1)

        @pl.when(is_scout & (ic > 1))
        def _():
            sent(direct + 2 + 2 * (nc - 1 - ic) + 1 - lax.rem(ic, 2), 1)

    def stages(ends, ahead=False, done=()):
        ends = [end for end in ends if end < steps] + list(range(slots, steps + 1, slots))
        step = filled = 0
        for end in sorted(set(ends + [steps])):
            if end == steps:
                wait_sent()
            order = list(range(max(filled, 1), min(slots, steps) if ahead and end < slots else end))
            if 1 in order and 2 in order and not ahead:
                order[0:2] = [2, 1]
            for n in order:
                if n not in done:
                    fill(n)
            filled = max([filled] + [n + 1 for n in order])
            use(step, end - step)
            step = end

    @pl.when(is_scout & outer)
    def _():
        stages([3])

    @pl.when(is_hub & outer)
    def _():
        stages([2], done={1})

    @pl.when(is_scout & (mine > 0) & (mine < steps - 1))
    def _():
        stages([2], ahead=True)

    @pl.when(mine == 0)
    def _():
        stages([2, 3])

    @pl.when(is_hub & (mine > 0) & (mine < steps - 1))
    def _():
        stages([2])


    @pl.when(is_scout & (ic == 0))
    def _():
        sent(1 + 2 * (nc - 2) + jnp.minimum(chip, 1), nc - 1)

    @pl.when(is_scout & (ic + chip > 0))
    def _():
        def one(j):
            wait_for(gath_c.at[pl.ds(0, 2)], local)
            wait_for(gath_ce.at[pl.ds(0, 2)], local)

        each(mine + 1, steps, one)


def per_device(val_orbitals, cond_orbitals, val_energy, cond_energy, wave_index):
    nv, nc = lax.axis_size("val"), lax.axis_size("cond")
    vb, points = val_orbitals.shape
    cb = cond_orbitals.shape[0]
    count = wave_index.shape[0]
    rows = NW // nv
    steps = nc // 2
    slots = min(4, steps)
    height = nv * vb * 2 * cb
    bf16, f32 = jnp.bfloat16, jnp.float32
    dma = pltpu.SemaphoreType.DMA
    regular = pltpu.SemaphoreType.REGULAR
    out = pl.pallas_call(
        functools.partial(kernel, nv, nc, slots),
        out_shape=jax.ShapeDtypeStruct((2 * rows, count), f32),
        in_specs=[pl.BlockSpec(memory_space=pltpu.HBM)] * 5,
        out_specs=pl.BlockSpec(memory_space=pltpu.VMEM),
        scratch_shapes=[
            pltpu.VMEM((nv, vb, points), bf16),
            pltpu.VMEM((nc, cb, points), bf16),
            pltpu.VMEM((nv, 1, vb), bf16),
            pltpu.VMEM((nc, 1, cb), bf16),
            pltpu.VMEM((count // LANES, LANES), jnp.int32),
            pltpu.VMEM((1, LANES), jnp.int32),
            pltpu.VMEM((points, count), bf16),
            pltpu.VMEM((points, count), bf16),
            pltpu.VMEM((2 * rows, points), bf16),
            pltpu.VMEM((slots * height, points), bf16),
            pltpu.VMEM((8, slots * height), f32),
            pltpu.VMEM((2 * rows, points), f32),
            dma, dma, dma((steps,)), dma((steps,)), dma, dma, regular((nc,)), dma,
        ],
        compiler_params=pltpu.CompilerParams(
            collective_id=0, has_side_effects=True, vmem_limit_bytes=VMEM_LIMIT
        ),
    )(*[
        pltpu.with_memory_space_constraint(value, pltpu.HBM)
        for value in (
            val_orbitals, cond_orbitals, val_energy.reshape(1, vb), cond_energy.reshape(1, cb),
            wave_index.reshape(count // LANES, LANES),
        )
    ])
    factor = -4.0 / math.sqrt(nv * vb * nc * cb)
    return factor * out[0:rows], factor * out[rows:2 * rows]


def solution(mesh):
    return jax.shard_map(
        per_device,
        mesh=mesh,
        in_specs=(P("val", None), P("cond", None), P("val"), P("cond"), P("cond")),
        out_specs=(P("val", "cond"), P("val", "cond")),
        check_vma=False,
    )
```
